256 devices in a mesh: space: 32 (over z, y_lo, core), tm: 4 (over x), cores: 2 (over y_hi).
Axes of the slice: x: 4, y: 4 (y_hi: 2, y_lo: 2; y = y_hi * 2 + y_lo), z: 8, core: 2. Of those that a mesh axis runs over, the one named last changes fastest.
Arguments:
- initial_state: float32 [1024, 64, 512], P('space', 'cores'), may hold values from -6 to 6
- heat_source: float32 [1024, 64, 512], P('space', 'cores'), may hold values from -3 to 3
- source_amplitude: float32 [32], P('tm'), may hold values from 0.5 to 1.5
- diffusivity: float32 [32], P('space'), may hold values from 0.5 to 2
- robin_param: float32 [32], P('space'), may hold values from 0.5 to 4
- spectrum_x: float32 [32], replicated, may hold values from 0.002 to 0.38
- spectrum_y: float32 [64], P('cores'), may hold values from 0.002 to 0.38
- spectrum_z: float32 [512], replicated, may hold values from 0.002 to 0.38
- robin_in: float32 [32, 2, 32, 64, 512], P('space', None, 'tm', 'cores'), may hold values from -8 to 8
- open_flag: int32 [32, 64], P(None, 'cores'), may hold values from 0 to 1, as said below
- owner_side: int32 [32, 64], P(None, 'cores'), may hold values from 0 to 1, as said below
Outputs:
- robin_out: float32 [32, 2, 32, 64, 512], P('space', None, 'tm', 'cores')
- window_end: float32 [4, 1024, 64, 512], P('tm', 'space', 'cores')
The draws below stay inside these ranges and needn't reach their ends.
Inputs may be any that keep to these rules, and one draw needn't show every extreme that they name: In each aligned group of 4 modes b of an interface exactly one has open_flag 0. In each aligned pair of modes b of an interface exactly one has owner_side 1.
All inputs are finite; a program needn't handle non-finite values.
Results may differ from the reference program's by a relative error of at most 0.00015.
Values sent between devices are 32-bit elements; how exact they have to be, the bound alone decides.
A program may use at most 128 MiB of HBM per device.

```python
import math
import jax
import jax.numpy as jnp
from jax import lax

NX = 32
NY = 64
NZ = 512
STEPS = 8
SUBDOMAINS = 32
LENGTH = 1024
MOMENTS = 32
N_SPACE = 32
N_TM = 4


def draw_open_flag(key, part):
    closed_at = jax.random.randint(jax.random.fold_in(key, 11), (SUBDOMAINS, NY // 4), 0, 4)
    slots = jnp.arange(4, dtype=jnp.int32)[None, None, :]
    return (slots != closed_at[:, :, None]).astype(jnp.int32).reshape(SUBDOMAINS, NY)


def draw_owner_side(key, part):
    right_at = jax.random.randint(jax.random.fold_in(key, 23), (SUBDOMAINS, NY // 2), 0, 2)
    slots = jnp.arange(2, dtype=jnp.int32)[None, None, :]
    return (slots == right_at[:, :, None]).astype(jnp.int32).reshape(SUBDOMAINS, NY)


def block_levels(stream_key, extent, pieces, low, high):
    gain, own = 1.0, jax.random.fold_in(stream_key, 6)
    for axis_at, parts in pieces:
        steps = jnp.exp(jax.random.uniform(jax.random.fold_in(own, axis_at), (parts,), jnp.float32, low / len(pieces), high / len(pieces)))
        gain = gain * jnp.repeat(steps, extent[axis_at] // parts).reshape([-1 if axis == axis_at else 1 for axis in range(len(extent))])
    return gain


def gaussian(stream_key, shape, width, bound, pieces=(), kind=jnp.bfloat16):
    values = width * jax.random.normal(stream_key, shape, jnp.float32)
    if pieces:
        values = values * block_levels(stream_key, shape, pieces, -0.22, 0.18)
    return jnp.clip(values, -bound, bound).astype(kind)


def setup_inputs(seed: int = 0) -> dict:
    seeds = jax.random.split(jax.random.key(seed), 12)
    initial_state = gaussian(seeds[0], (LENGTH, NY, NZ), 1.0, 6.0, ((0, 32), (1, 2)), jnp.float32)
    heat_source = gaussian(seeds[1], (LENGTH, NY, NZ), 0.2, 3.0, ((0, 32), (1, 2)), jnp.float32)
    source_amplitude = jnp.clip(0.5 + 1.0 * jax.random.uniform(seeds[2], (MOMENTS,), jnp.float32) ** block_levels(seeds[2], (MOMENTS,), ((0, 4),), -0.2, 0.2), 0.5, 1.5)
    diffusivity = jnp.clip(jnp.exp(math.log(2.0) - 1.3862944 * jax.random.uniform(seeds[3], (SUBDOMAINS,), jnp.float32) ** block_levels(seeds[3], (SUBDOMAINS,), ((0, 32),), -0.2, 0.2)), 0.5, 2.0)
    robin_param = jnp.clip(jnp.exp(math.log(4.0) - 2.0794415 * jax.random.uniform(seeds[4], (SUBDOMAINS,), jnp.float32) ** block_levels(seeds[4], (SUBDOMAINS,), ((0, 32),), -0.2, 0.2)), 0.5, 4.0)
    spectrum_x = jnp.clip(jnp.exp(jax.random.uniform(seeds[5], (NX,), jnp.float32, math.log(0.002), math.log(0.38))), 0.002, 0.38)
    spectrum_y = jnp.clip(jnp.exp(math.log(0.38) - 5.247024 * jax.random.uniform(seeds[6], (NY,), jnp.float32) ** block_levels(seeds[6], (NY,), ((0, 2),), -0.2, 0.2)), 0.002, 0.38)
    spectrum_z = jnp.clip(jnp.exp(jax.random.uniform(seeds[7], (NZ,), jnp.float32, math.log(0.002), math.log(0.38))), 0.002, 0.38)
    robin_in = gaussian(seeds[8], (SUBDOMAINS, 2, MOMENTS, NY, NZ), 2.0, 8.0, ((0, 32), (2, 4), (3, 2)), jnp.float32)
    open_flag = draw_open_flag(jax.random.fold_in(seeds[11], 71), 0)
    owner_side = draw_owner_side(jax.random.fold_in(seeds[11], 71), 0)
    return {"initial_state": initial_state, "heat_source": heat_source, "source_amplitude": source_amplitude, "diffusivity": diffusivity, "robin_param": robin_param, "spectrum_x": spectrum_x, "spectrum_y": spectrum_y, "spectrum_z": spectrum_z, "robin_in": robin_in, "open_flag": open_flag, "owner_side": owner_side}


HIGHEST = lax.Precision.HIGHEST

def cosine_basis(order):
    mode_rows = jnp.arange(order, dtype=jnp.float32)[:, None]
    node_cols = jnp.arange(order, dtype=jnp.float32)[None, :]
    scaling = jnp.where(mode_rows == 0, jnp.sqrt(1.0 / order), jnp.sqrt(2.0 / order))
    return (scaling * jnp.cos(jnp.pi * mode_rows * (node_cols + 0.5) / order)).astype(jnp.float32)

def reference(initial_state, heat_source, source_amplitude, diffusivity, robin_param, spectrum_x, spectrum_y, spectrum_z, robin_in, open_flag, owner_side):
    subdomains = N_SPACE
    basis_x = cosine_basis(NX)
    basis_y = cosine_basis(NY)
    basis_z = cosine_basis(NZ)

    def forward(values):
        values = jnp.einsum('ax,sxyz->sayz', basis_x, values, precision=HIGHEST)
        values = jnp.einsum('by,sayz->sabz', basis_y, values, precision=HIGHEST)
        return jnp.einsum('cz,sabz->sabc', basis_z, values, precision=HIGHEST)

    def inverse(spectral):
        values = jnp.einsum('ax,sabc->sxbc', basis_x, spectral, precision=HIGHEST)
        values = jnp.einsum('by,sxbc->sxyc', basis_y, values, precision=HIGHEST)
        return jnp.einsum('cz,sxyc->sxyz', basis_z, values, precision=HIGHEST)
    current = forward(initial_state.reshape(subdomains, NX, NY, NZ))
    source_modes = forward(heat_source.reshape(subdomains, NX, NY, NZ))
    rates = spectrum_x[:, None, None] + spectrum_y[None, :, None] + spectrum_z[None, None, :]
    factor = 1.0 / (1.0 + diffusivity[:, None, None, None] * rates[None])
    edge_rows = jnp.stack([basis_x[:, 0], basis_x[:, 1] - basis_x[:, 0], basis_x[:, NX - 1], basis_x[:, NX - 1] - basis_x[:, NX - 2]])
    owners = (jnp.arange(subdomains, dtype=jnp.int32)[:, None] + owner_side) % subdomains
    weight = robin_param[owners][:, :, None]
    opened = open_flag.astype(jnp.float32)[:, :, None]
    left_col = basis_x[:, 0][None, :, None, None]
    right_col = basis_x[:, NX - 1][None, :, None, None]
    robin_steps = []
    window_ends = []
    for window in range(N_TM):
        for substep in range(STEPS):
            moment = window * STEPS + substep
            forcing = current + source_amplitude[moment] * source_modes
            forcing = forcing + left_col * robin_in[:, 0, moment][:, None] + right_col * robin_in[:, 1, moment][:, None]
            current = forcing * factor
            traces = jnp.einsum('ka,sabc->ksbc', edge_rows, current, precision=HIGHEST)
            right_data = opened * (jnp.roll(traces[1], -1, 0) + weight * jnp.roll(traces[0], -1, 0))
            left_data = jnp.roll(opened * (weight * traces[2] - traces[3]), 1, 0)
            robin_steps.append(jnp.stack([left_data, right_data], axis=1))
        window_ends.append(inverse(current))
    robin_out = jnp.stack(robin_steps, axis=2)
    window_end = jnp.stack(window_ends).reshape(N_TM, subdomains * NX, NY, NZ)
    return (robin_out, window_end)
```

```python
import functools

import jax
import jax.numpy as jnp
import ml_dtypes
import numpy as np
from jax import lax
from jax.experimental import pallas as pl
from jax.experimental.pallas import tpu as pltpu
from jax.sharding import PartitionSpec as P

MESH = pl.DeviceIdType.MESH
F32, BF16 = jnp.float32, jnp.bfloat16
NX, NY, NZ, STEPS, TM, SPACE = 32, 64, 512, 8, 4, 32
CB = NZ // TM
PERM = list(range(0, NX, 2)) + list(range(1, NX, 2))


def cosine(n):
    k = np.arange(n)[:, None]
    i = np.arange(n)[None, :]
    scale = np.where(k == 0, np.sqrt(1.0 / n), np.sqrt(2.0 / n))
    return scale * np.cos(np.pi * k * (i + 0.5) / n)


C_X, C_Y, C_Z = cosine(NX), cosine(NY), cosine(NZ)
EDGE = C_X[PERM, 0]
VALUE_W = [float(v) for v in EDGE * EDGE]
SLOPE_W = [float(v) for v in (C_X[PERM, 1] - C_X[PERM, 0]) * EDGE]


def split_constant(m):
    hi = np.asarray(m, np.float32).astype(ml_dtypes.bfloat16)
    lo = (np.asarray(m, np.float64) - hi.astype(np.float64)).astype(np.float32)
    return np.stack([hi, lo.astype(ml_dtypes.bfloat16)])


def constants():
    eye8, eye4 = np.eye(8), np.eye(4)
    x_fwd = np.kron(C_X[PERM] / EDGE[:, None], eye8)
    x_inv = np.kron((C_X[PERM] * EDGE[:, None]).T, eye8)
    cy = C_Y.reshape(8, 8, 8, 8)
    y_fwd = np.einsum("pbqy,ac->pabqcy", cy, eye4).reshape(256, 256)
    y_inv = np.einsum("pbqy,ac->qaypcb", cy, eye4).reshape(2, 128, 256)
    y_inv = np.stack([split_constant(y_inv[0]), split_constant(y_inv[1])])
    z_fwd = split_constant(C_Z.T)
    z_fwd = z_fwd.reshape(2, NZ, TM, CB).transpose(2, 1, 0, 3).reshape(TM, NZ, 2 * CB)
    z_inv = split_constant(C_Z).reshape(2, TM, CB, NZ)
    return (split_constant(x_fwd), split_constant(y_fwd), y_inv, split_constant(x_inv), z_fwd, z_inv)


def split(v):
    hi = v.astype(BF16)
    return hi, (v - hi.astype(F32)).astype(BF16)


def dot(a, b):
    return jnp.dot(a, b, preferred_element_type=F32)


def const_dot(m_hi, m_lo, v):
    hi, lo = split(v)
    return dot(m_hi, hi) + (dot(m_lo, hi) + dot(m_hi, lo))


def sweep_kernel(
    state_in, heat_in, robin_in, zf_in,
    amp_s, diff_s, param_s, specx_s, specy, specz, flag, owner,
    xf, yf, yi, xi, zi,
    robin_out, ends_out,
    xin, zf, v, sycol, ptile, amp, rb, modes, src, fac, tr, coef, ob, tbuf, ubuf, wr, acc,
    s_in, s_zf, s_rl, s_rs, r_rb, s_ro, s_f, r_f, s_y, r_y, s_p, r_p, s_a, r_a,
    s_o, r_o, s_w, r_w, s_out,
):
    s = lax.axis_index("space")
    w = lax.axis_index("tm")
    h = lax.axis_index("cores")
    oh = 1 - h
    left = lax.rem(s + SPACE - 1, SPACE)
    right = lax.rem(s + 1, SPACE)

    def remote(a, b, ss, rs, to):
        return pltpu.make_async_remote_copy(
            src_ref=a, dst_ref=b, send_sem=ss, recv_sem=rs, device_id=to, device_id_type=MESH
        )

    def other(d):
        return lax.rem(w + d, TM)

    ins = (state_in, heat_in)
    zf_copy = pltpu.make_async_copy(zf_in.at[w], zf, s_zf)
    zf_copy.start()

    def load(i, yt):
        rows = pl.ds(pl.multiple_of(yt * 8, 8), 8)
        return pltpu.make_async_copy(ins[i].at[:, rows, :], xin.at[i, :, rows, :], s_in.at[i, yt])

    for yt in range(4):
        for i in range(2):
            load(i, yt).start()

    def robin_block(d):
        return robin_in.at[0, :, :, :, pl.ds(pl.multiple_of(d * CB, CB), CB)]

    own_robin = pltpu.make_async_copy(robin_block(w), rb.at[h, w], s_rl)
    own_robin.start()

    barrier = pltpu.get_barrier_semaphore()
    for d in range(1, TM):
        pl.semaphore_signal(barrier, inc=1, device_id=(s, other(d), h), device_id_type=MESH)
    for d in range(TM):
        pl.semaphore_signal(barrier, inc=1, device_id=(s, other(d), oh), device_id_type=MESH)
        pl.semaphore_signal(barrier, inc=1, device_id=(left, other(d), h), device_id_type=MESH)
        pl.semaphore_signal(barrier, inc=1, device_id=(right, other(d), h), device_id_type=MESH)

    def column(row):
        n = row.shape[1]
        on = lax.broadcasted_iota(jnp.int32, (n, n), 0) == lax.broadcasted_iota(jnp.int32, (n, n), 1)
        picked = jnp.where(on, jnp.broadcast_to(row, (n, n)), 0.0)
        return jnp.broadcast_to(jnp.sum(picked, axis=1, keepdims=True), (n, CB))

    for j in range(STEPS):
        amp[w, j] = jnp.full((8, CB), amp_s[j], F32)
    ptile[1] = jnp.full((8, CB), param_s[0], F32)
    sycol[h] = column(specy[...])
    pl.semaphore_wait(barrier, 15)

    small = [
        remote(sycol.at[h], sycol.at[h], s_y, r_y, (s, w, oh)),
        remote(ptile.at[1], ptile.at[0], s_p.at[0], r_p.at[0], (right, w, h)),
        remote(ptile.at[1], ptile.at[2], s_p.at[1], r_p.at[1], (left, w, h)),
    ]
    for d in range(1, TM):
        small.append(remote(amp.at[w], amp.at[w], s_a.at[d], r_a.at[w], (s, other(d), h)))
    for c in small:
        c.start()
    same_half = []
    for d in range(1, TM):
        c = remote(robin_block(other(d)), rb.at[h, w], s_rs.at[d], r_rb.at[h, w], (s, other(d), h))
        c.start()
        same_half.append(c)

    def fwd_send(yt):
        return remote(v.at[h, yt], v.at[h, yt], s_f.at[yt], r_f.at[yt], (s, w, oh))

    zf_copy.wait()

    def fwd_chunk(yt, carry):
        rows = pl.ds(pl.multiple_of(yt * 8, 8), 8)
        zs = []
        for i in range(2):
            load(i, yt).wait()
            hi, lo = split(xin[i, :, rows, :].reshape(NX * 8, NZ))
            both = dot(hi, zf[...])
            zs.append(both[:, :CB] + (both[:, CB:] + dot(lo, zf[:, :CB])))
        res = const_dot(xf[0], xf[1], jnp.concatenate(zs, axis=1))
        v[h, yt, 0] = res[:, :CB].reshape(NX, 8, CB)
        v[h, yt, 1] = res[:, CB:].reshape(NX, 8, CB)
        fwd_send(yt).start()
        return carry

    lax.fori_loop(0, 4, fwd_chunk, 0)

    pl_copy = small
    for c in pl_copy[:3]:
        c.wait_send()
    remote(sycol.at[oh], sycol.at[oh], s_y, r_y, (s, w, oh)).wait_recv()
    small[1].wait_recv()
    small[2].wait_recv()

    def coefficient(at, here, beyond):
        opened = column(flag[pl.ds(at, 1), :].astype(F32))
        side = column(owner[pl.ds(at, 1), :].astype(F32))
        p = jnp.where(side > 0.5, beyond, here)
        return opened, opened * p

    pt = [jnp.broadcast_to(ptile[i][0:1], (32, CB)) for i in range(3)]
    o_l, op_l = coefficient(left, pt[0], pt[1])
    o_r, op_r = coefficient(s, pt[1], pt[2])
    coef[0] = o_l
    coef[1] = op_l
    coef[2] = o_r
    coef[3] = op_r

    sz = jnp.broadcast_to(specz[:, pl.ds(pl.multiple_of(w * CB, CB), CB)], (8, CB))

    def factor(bt, carry):
        sy = sycol[lax.div(bt, 4), pl.ds(pl.multiple_of(lax.rem(bt, 4) * 8, 8), 8), :]
        for a in range(NX):
            rate = (specx_s[PERM[a]] + sy) + sz
            fac[bt, a] = 1.0 / (1.0 + diff_s[0] * rate)
        return carry

    lax.fori_loop(0, 8, factor, 0)

    for yt in range(4):
        fwd_send(yt).wait_send()
    def cross(d):
        return remote(robin_block(other(d)), rb.at[h, w], s_ro.at[d], r_rb.at[h, w], (s, other(d), oh))

    for d in range(TM):
        cross(d).start()

    for yt in range(4):
        remote(v.at[oh, yt], v.at[oh, yt], s_f.at[yt], r_f.at[yt], (s, w, oh)).wait_recv()

    def y_forward(g, carry):
        at = pl.ds(g * 4, 4)
        rhs = jnp.concatenate([v[:, :, i, at].reshape(256, CB) for i in range(2)], axis=1)
        res = const_dot(yf[0], yf[1], rhs)
        modes[0, :, at] = res[:, :CB].reshape(8, 4, 8, CB)
        src[:, at] = res[:, CB:].reshape(8, 4, 8, CB)
        return carry

    lax.fori_loop(0, 8, y_forward, 0)

    own_robin.wait()
    for d in range(1, TM):
        f = other(d)
        remote(rb.at[h, f], rb.at[h, f], s_rs.at[d], r_rb.at[h, f], (s, f, h)).wait_recv()
        remote(amp.at[f], amp.at[f], s_a.at[d], r_a.at[f], (s, f, h)).wait_recv()

    def steps(k, half, bt, traces):
        tile = half * 4 + bt
        rows = pl.ds(pl.multiple_of(bt * 8, 8), 8)
        for g in range(4):
            a0 = g * 8
            mu = [modes[k, tile, a0 + i] for i in range(8)]
            fs = [fac[tile, a0 + i] for i in range(8)]
            sg = [src[tile, a0 + i] for i in range(8)]
            for j in range(STEPS):
                r0 = rb[half, k, 0, j, rows, :]
                r1 = rb[half, k, 1, j, rows, :]
                p = r0 + r1 if g < 2 else r0 - r1
                am = amp[k, j]
                for i in range(8):
                    mu[i] = (mu[i] + (am * sg[i] + p)) * fs[i]
                if traces:
                    val = [VALUE_W[a0 + i] * mu[i] for i in range(8)]
                    slo = [SLOPE_W[a0 + i] * mu[i] for i in range(8)]
                    val = sum(val[1:], val[0])
                    slo = sum(slo[1:], slo[0])
                    if g % 2 == 0:
                        tr[j, g] = val
                        tr[j, g + 1] = slo
                    elif g == 1:
                        tr[j, 0] += val
                        tr[j, 1] += slo
                    else:
                        e0, e1 = tr[j, 0], tr[j, 1]
                        o0 = tr[j, 2] + val
                        o1 = tr[j, 3] + slo
                        at = k * STEPS + j
                        ob[1, at, rows, :] = coef[0, rows, :] * (e1 + o1) + coef[1, rows, :] * (e0 + o0)
                        ob[0, at, rows, :] = coef[3, rows, :] * (e0 - o0) - coef[2, rows, :] * (o1 - e1)
            for i in range(8):
                modes[k + 1, tile, a0 + i] = mu[i]

    def own_steps(t, carry):
        k, bt = lax.div(t, 4), lax.rem(t, 4)
        steps(k, h, bt, True)
        return carry

    def robin_send(side, k):
        to = left if side == 1 else right
        return remote(
            ob.at[side, pl.ds(pl.multiple_of(k * STEPS, STEPS), STEPS)],
            robin_out.at[0, side, :, :, pl.ds(pl.multiple_of(w * CB, CB), CB)],
            s_o.at[side, k], r_o.at[side, w], (to, k, h),
        )

    def own_window(k, carry):
        lax.fori_loop(k * 4, k * 4 + 4, own_steps, 0)
        robin_send(0, k).start()
        robin_send(1, k).start()
        return carry

    lax.fori_loop(0, TM, own_window, 0)

    def end_send(k):
        return remote(ubuf.at[k], wr.at[w], s_w.at[k], r_w.at[w], (s, k, h))

    def other_window(k, carry):
        remote(rb.at[oh, k], rb.at[oh, k], s_ro.at[0], r_rb.at[oh, k], (s, k, oh)).wait_recv()

        def body(bt, c):
            steps(k, oh, bt, False)
            return c

        lax.fori_loop(0, 4, body, 0)
        my_hi, my_lo = yi[h, 0], yi[h, 1]

        def y_inverse(g, c):
            a, b = pl.ds(g * 8, 4), pl.ds(g * 8 + 4, 4)
            rhs = jnp.concatenate(
                [modes[k + 1, :, a].reshape(256, CB), modes[k + 1, :, b].reshape(256, CB)], axis=1
            )
            res = const_dot(my_hi, my_lo, rhs)
            tbuf[:, a] = res[:, :CB].reshape(4, 4, 8, CB)
            tbuf[:, b] = res[:, CB:].reshape(4, 4, 8, CB)
            return c

        lax.fori_loop(0, 4, y_inverse, 0)

        def x_inverse(q, c):
            rhs = jnp.concatenate(
                [tbuf[2 * q].reshape(256, CB), tbuf[2 * q + 1].reshape(256, CB)], axis=1
            )
            res = const_dot(xi[0], xi[1], rhs)
            ubuf[k, 2 * q] = res[:, :CB].reshape(NX, 8, CB)
            ubuf[k, 2 * q + 1] = res[:, CB:].reshape(NX, 8, CB)
            return c

        lax.fori_loop(0, 2, x_inverse, 0)

        @pl.when(k != w)
        def _():
            end_send(k).start()

        return carry

    lax.fori_loop(0, TM, other_window, 0)

    def z_inverse(ref, index, b, first):
        def body(yt, c):
            hi, lo = split(ref[index, yt].reshape(NX * 8, CB))
            m_hi, m_lo = zi[0, b], zi[1, b]
            part = (dot(hi, m_hi) + (dot(lo, m_hi) + dot(hi, m_lo))).reshape(NX, 8, NZ)
            if first:
                acc[yt] = part
            else:
                acc[yt] += part
            return c

        lax.fori_loop(0, 4, body, 0)

    z_inverse(ubuf, w, w, True)
    for d in (1, 3, 2):
        f = other(d)
        remote(ubuf.at[f], wr.at[f], s_w.at[f], r_w.at[f], (s, f, h)).wait_recv()
        z_inverse(wr, f, f, False)

    def store(yt):
        rows = pl.ds(pl.multiple_of(yt * 8, 8), 8)
        return pltpu.make_async_copy(acc.at[yt], ends_out.at[0, :, rows, :], s_out.at[yt])

    for yt in range(4):
        store(yt).start()

    for c in small[3:]:
        c.wait_send()
    for c in same_half:
        c.wait_send()
    for d in range(TM):
        cross(d).wait_send()
    for k in range(TM):
        for side in range(2):
            robin_send(side, k).wait_send()
    for d in range(1, TM):
        end_send(other(d)).wait_send()
    for k in range(TM):
        for side in range(2):
            remote(
                ob.at[side, pl.ds(k * STEPS, STEPS)],
                robin_out.at[0, side, :, :, pl.ds(k * CB, CB)],
                s_o.at[side, k], r_o.at[side, k], (left, k, h),
            ).wait_recv()
    for yt in range(4):
        store(yt).wait()


def local(
    initial_state, heat_source, source_amplitude, diffusivity, robin_param,
    spectrum_x, spectrum_y, spectrum_z, robin_in, open_flag, owner_side,
):
    xf, yf, yi, xi, zf, zi = (jnp.asarray(c) for c in constants())
    any_spec = pl.BlockSpec(memory_space=pl.ANY)
    smem = pl.BlockSpec(memory_space=pltpu.SMEM)
    vmem = pl.BlockSpec(memory_space=pltpu.VMEM)
    dma = pltpu.SemaphoreType.DMA
    tile = (8, CB)
    return pl.pallas_call(
        sweep_kernel,
        out_shape=(
            jax.ShapeDtypeStruct((1, 2, STEPS, 32, NZ), F32),
            jax.ShapeDtypeStruct((1, NX, 32, NZ), F32),
        ),
        in_specs=[any_spec] * 4 + [smem] * 4 + [vmem] * 9,
        out_specs=(any_spec, any_spec),
        scratch_shapes=[
            pltpu.VMEM((2, NX, 32, NZ), F32),
            pltpu.VMEM((NZ, 2 * CB), BF16),
            pltpu.VMEM((2, 4, 2, NX) + tile, F32),
            pltpu.VMEM((2, 32, CB), F32),
            pltpu.VMEM((3,) + tile, F32),
            pltpu.VMEM((TM, STEPS) + tile, F32),
            pltpu.VMEM((2, TM, 2, STEPS, 32, CB), F32),
            pltpu.VMEM((TM + 1, 8, NX) + tile, F32),
            pltpu.VMEM((8, NX) + tile, F32),
            pltpu.VMEM((8, NX) + tile, F32),
            pltpu.VMEM((STEPS, 4) + tile, F32),
            pltpu.VMEM((4, 32, CB), F32),
            pltpu.VMEM((2, TM * STEPS, 32, CB), F32),
            pltpu.VMEM((4, NX) + tile, F32),
            pltpu.VMEM((TM, 4, NX) + tile, F32),
            pltpu.VMEM((TM, 4, NX) + tile, F32),
            pltpu.VMEM((4, NX, 8, NZ), F32),
            dma((2, 4)), dma, dma, dma((TM,)), dma((2, TM)), dma((TM,)),
            dma((4,)), dma((4,)), dma, dma, dma((2,)), dma((2,)), dma((TM,)), dma((TM,)),
            dma((2, TM)), dma((2, TM)), dma((TM,)), dma((TM,)), dma((4,)),
        ],
        compiler_params=pltpu.CompilerParams(
            collective_id=0, has_side_effects=True, vmem_limit_bytes=52 << 20
        ),
        name="sweep",
    )(
        initial_state, heat_source, robin_in, zf,
        source_amplitude, diffusivity, robin_param, spectrum_x,
        spectrum_y[None], spectrum_z[None], open_flag, owner_side,
        xf, yf, yi, xi, zi,
    )


def solution(mesh):
    placed = (
        P("space", "cores", None),
        P("space", "cores", None),
        P("tm"),
        P("space"),
        P("space"),
        P(),
        P("cores"),
        P(),
        P("space", None, "tm", "cores", None),
        P(None, "cores"),
        P(None, "cores"),
    )
    return jax.shard_map(
        local,
        mesh=mesh,
        in_specs=placed,
        out_specs=(P("space", None, "tm", "cores", None), P("tm", "space", "cores", None)),
        check_vma=False,
    )
```

```python
import functools

import jax
import jax.numpy as jnp
import ml_dtypes
import numpy as np
from jax import lax
from jax.experimental import pallas as pl
from jax.experimental.pallas import tpu as pltpu
from jax.sharding import PartitionSpec as P

MESH = pl.DeviceIdType.MESH
F32, BF16 = jnp.float32, jnp.bfloat16
NX, NY, NZ, STEPS, TM, SPACE = 32, 64, 512, 8, 4, 32
CB = NZ // TM
PERM = list(range(0, NX, 2)) + list(range(1, NX, 2))


def cosine(n):
    k = np.arange(n)[:, None]
    i = np.arange(n)[None, :]
    scale = np.where(k == 0, np.sqrt(1.0 / n), np.sqrt(2.0 / n))
    return scale * np.cos(np.pi * k * (i + 0.5) / n)


C_X, C_Y, C_Z = cosine(NX), cosine(NY), cosine(NZ)
EDGE = C_X[PERM, 0]
VALUE_W = [float(v) for v in EDGE * EDGE]
SLOPE_W = [float(v) for v in (C_X[PERM, 1] - C_X[PERM, 0]) * EDGE]


def split_constant(m):
    hi = np.asarray(m, np.float32).astype(ml_dtypes.bfloat16)
    lo = (np.asarray(m, np.float64) - hi.astype(np.float64)).astype(np.float32)
    return np.stack([hi, lo.astype(ml_dtypes.bfloat16)])


def constants():
    eye8, eye4 = np.eye(8), np.eye(4)
    x_fwd = np.kron(C_X[PERM] / EDGE[:, None], eye8)
    x_inv = np.kron((C_X[PERM] * EDGE[:, None]).T, eye8)
    cy = C_Y.reshape(8, 8, 8, 8)
    y_fwd = np.einsum("pbqy,ac->pabqcy", cy, eye4).reshape(256, 256)
    y_inv = np.einsum("pbqy,ac->qaypcb", cy, eye4).reshape(2, 128, 256)
    y_inv = np.stack([split_constant(y_inv[0]), split_constant(y_inv[1])])
    z_fwd = split_constant(C_Z.T)
    z_fwd = z_fwd.reshape(2, NZ, TM, CB).transpose(2, 1, 0, 3).reshape(TM, NZ, 2 * CB)
    z_inv = split_constant(C_Z).reshape(2, TM, CB, NZ)
    return (split_constant(x_fwd), split_constant(y_fwd), y_inv, split_constant(x_inv), z_fwd, z_inv)


def split(v):
    hi = v.astype(BF16)
    return hi, (v - hi.astype(F32)).astype(BF16)


def dot(a, b):
    return jnp.dot(a, b, preferred_element_type=F32)


def const_dot(m_hi, m_lo, v):
    hi, lo = split(v)
    return dot(m_hi, hi) + (dot(m_lo, hi) + dot(m_hi, lo))


def sweep_kernel(
    state_in, heat_in, robin_in, zf_in,
    amp_in, diff_in, param_in, specx_in, specy_in, specz_in, flag_in, owner_in,
    xf_in, yf_in, yi_in, xi_in, zi_in,
    robin_out, ends_out,
    amp_s, diff_s, param_s, specx_s, specy, specz, flag, owner,
    xf, yf, yi, xi, zi,
    xin, zf, v, sycol, ptile, amp, rb, modes, src, fac, tr, coef, ob, st, tbuf, ubuf, wr, acc,
    s_c, s_in, s_zf, s_rl, s_rs, r_rb, s_ro, s_f, r_f, s_y, r_y, s_p, r_p, s_a, r_a,
    s_1, r_1, s_1l, s_o, r_o, s_w, r_w, s_out,
):
    s = lax.axis_index("space")
    w = lax.axis_index("tm")
    h = lax.axis_index("cores")
    oh = 1 - h
    left = lax.rem(s + SPACE - 1, SPACE)
    right = lax.rem(s + 1, SPACE)

    def remote(a, b, ss, rs, to):
        return pltpu.make_async_remote_copy(
            src_ref=a, dst_ref=b, send_sem=ss, recv_sem=rs, device_id=to, device_id_type=MESH
        )

    def other(d):
        return lax.rem(w + d, TM)

    ins = (state_in, heat_in)
    zf_copy = pltpu.make_async_copy(zf_in.at[w], zf, s_zf)
    zf_copy.start()
    operands = (
        (amp_in, amp_s), (param_in, param_s), (specy_in, specy), (xf_in, xf), (diff_in, diff_s),
        (specx_in, specx_s), (specz_in, specz), (flag_in, flag), (owner_in, owner),
        (yf_in, yf), (yi_in, yi), (xi_in, xi), (zi_in, zi),
    )
    loads = [pltpu.make_async_copy(a, b, s_c.at[i]) for i, (a, b) in enumerate(operands)]
    for c in loads[:4]:
        c.start()

    def load(i, yt):
        rows = pl.ds(pl.multiple_of(yt * 8, 8), 8)
        return pltpu.make_async_copy(ins[i].at[:, rows, :], xin.at[i, :, rows, :], s_in.at[i, yt])

    for yt in range(4):
        for i in range(2):
            load(i, yt).start()

    def robin_block(d):
        return robin_in.at[0, :, :, :, pl.ds(pl.multiple_of(d * CB, CB), CB)]

    own_robin = pltpu.make_async_copy(robin_block(w), rb.at[h, w], s_rl)
    own_robin.start()
    for c in loads[4:]:
        c.start()

    barrier = pltpu.get_barrier_semaphore()
    for d in range(1, TM):
        pl.semaphore_signal(barrier, inc=1, device_id=(s, other(d), h), device_id_type=MESH)
    for to in ((s, w, oh), (left, w, h), (right, w, h)):
        pl.semaphore_signal(barrier, inc=1, device_id=to, device_id_type=MESH)

    def column(row):
        n = row.shape[1]
        on = lax.broadcasted_iota(jnp.int32, (n, n), 0) == lax.broadcasted_iota(jnp.int32, (n, n), 1)
        picked = jnp.where(on, jnp.broadcast_to(row, (n, n)), 0.0)
        return jnp.broadcast_to(jnp.sum(picked, axis=1, keepdims=True), (n, CB))

    for c in loads[:3]:
        c.wait()
    for j in range(STEPS):
        amp[w, j] = jnp.full((8, CB), amp_s[j], F32)
    ptile[1] = jnp.full((8, CB), param_s[0], F32)
    sycol[h] = column(specy[...])
    pl.semaphore_wait(barrier, 6)

    small = [
        remote(sycol.at[h], sycol.at[h], s_y, r_y, (s, w, oh)),
        remote(ptile.at[1], ptile.at[0], s_p.at[0], r_p.at[0], (right, w, h)),
        remote(ptile.at[1], ptile.at[2], s_p.at[1], r_p.at[1], (left, w, h)),
    ]
    for d in range(1, TM):
        small.append(remote(amp.at[w], amp.at[w], s_a.at[d], r_a.at[w], (s, other(d), h)))
    for c in small:
        c.start()
    same_half = []
    for d in range(1, TM):
        c = remote(robin_block(other(d)), rb.at[h, w], s_rs.at[d], r_rb.at[h, w], (s, other(d), h))
        c.start()
        same_half.append(c)

    def fwd_send(yt):
        return remote(v.at[h, yt], v.at[h, yt], s_f.at[yt], r_f.at[yt], (s, w, oh))

    zf_copy.wait()
    loads[3].wait()

    def fwd_chunk(yt, carry):
        rows = pl.ds(pl.multiple_of(yt * 8, 8), 8)
        zs = []
        for i in range(2):
            load(i, yt).wait()
            hi, lo = split(xin[i, :, rows, :].reshape(NX * 8, NZ))
            both = dot(hi, zf[...])
            zs.append(both[:, :CB] + (both[:, CB:] + dot(lo, zf[:, :CB])))
        res = const_dot(xf[0], xf[1], jnp.concatenate(zs, axis=1))
        v[h, yt, 0] = res[:, :CB].reshape(NX, 8, CB)
        v[h, yt, 1] = res[:, CB:].reshape(NX, 8, CB)
        fwd_send(yt).start()
        return carry

    lax.fori_loop(0, 4, fwd_chunk, 0)

    for c in loads[4:9]:
        c.wait()
    remote(sycol.at[oh], sycol.at[oh], s_y, r_y, (s, w, oh)).wait_recv()
    small[1].wait_recv()
    small[2].wait_recv()

    def coefficient(at, here, beyond):
        opened = column(flag[pl.ds(at, 1), :].astype(F32))
        side = column(owner[pl.ds(at, 1), :].astype(F32))
        p = jnp.where(side > 0.5, beyond, here)
        return opened, opened * p

    pt = [jnp.broadcast_to(ptile[i][0:1], (32, CB)) for i in range(3)]
    o_l, op_l = coefficient(left, pt[0], pt[1])
    o_r, op_r = coefficient(s, pt[1], pt[2])
    coef[0] = o_l
    coef[1] = op_l
    coef[2] = o_r
    coef[3] = op_r

    sz = jnp.broadcast_to(specz[:, pl.ds(pl.multiple_of(w * CB, CB), CB)], (8, CB))

    def factor(bt, carry):
        sy = sycol[lax.div(bt, 4), pl.ds(pl.multiple_of(lax.rem(bt, 4) * 8, 8), 8), :]
        for a in range(NX):
            rate = (specx_s[PERM[a]] + sy) + sz
            fac[bt, a] = 1.0 / (1.0 + diff_s[0] * rate)
        return carry

    lax.fori_loop(0, 8, factor, 0)

    for yt in range(4):
        fwd_send(yt).wait_send()
    own_robin.wait()
    for d in range(1, TM):
        f = other(d)
        remote(rb.at[h, f], rb.at[h, f], s_rs.at[d], r_rb.at[h, f], (s, f, h)).wait_recv()
        remote(amp.at[f], amp.at[f], s_a.at[d], r_a.at[f], (s, f, h)).wait_recv()

    def cross(k):
        return remote(rb.at[h, k], rb.at[h, k], s_ro.at[k], r_rb.at[h, k], (s, w, oh))

    for k in range(2):
        cross(k).start()
    for c in loads[9:]:
        c.wait()

    for yt in range(4):
        remote(v.at[oh, yt], v.at[oh, yt], s_f.at[yt], r_f.at[yt], (s, w, oh)).wait_recv()

    def y_forward(g, carry):
        at = pl.ds(g * 4, 4)
        rhs = jnp.concatenate([v[:, :, i, at].reshape(256, CB) for i in range(2)], axis=1)
        res = const_dot(yf[0], yf[1], rhs)
        modes[0, :, at] = res[:, :CB].reshape(8, 4, 8, CB)
        src[:, at] = res[:, CB:].reshape(8, 4, 8, CB)
        return carry

    lax.fori_loop(0, 8, y_forward, 0)

    def steps(k, half, bt, traces):
        tile = half * 4 + bt
        rows = pl.ds(pl.multiple_of(bt * 8, 8), 8)
        for g in range(4):
            a0 = g * 8
            mu = [modes[k, tile, a0 + i] for i in range(8)]
            fs = [fac[tile, a0 + i] for i in range(8)]
            sg = [src[tile, a0 + i] for i in range(8)]
            for j in range(STEPS):
                r0 = rb[half, k, 0, j, rows, :]
                r1 = rb[half, k, 1, j, rows, :]
                p = r0 + r1 if g < 2 else r0 - r1
                am = amp[k, j]
                for i in range(8):
                    mu[i] = (mu[i] + (am * sg[i] + p)) * fs[i]
                if traces:
                    val = [VALUE_W[a0 + i] * mu[i] for i in range(8)]
                    slo = [SLOPE_W[a0 + i] * mu[i] for i in range(8)]
                    val = sum(val[1:], val[0])
                    slo = sum(slo[1:], slo[0])
                    if g % 2 == 0:
                        tr[j, g] = val
                        tr[j, g + 1] = slo
                    elif g == 1:
                        tr[j, 0] += val
                        tr[j, 1] += slo
                    else:
                        e0, e1 = tr[j, 0], tr[j, 1]
                        o0 = tr[j, 2] + val
                        o1 = tr[j, 3] + slo
                        at = k * STEPS + j
                        ob[1, at, rows, :] = coef[0, rows, :] * (e1 + o1) + coef[1, rows, :] * (e0 + o0)
                        ob[0, at, rows, :] = coef[3, rows, :] * (e0 - o0) - coef[2, rows, :] * (o1 - e1)
            for i in range(8):
                modes[k + 1, tile, a0 + i] = mu[i]

    def own_steps(t, carry):
        k, bt = lax.div(t, 4), lax.rem(t, 4)
        steps(k, h, bt, True)
        return carry

    lanes = pl.ds(pl.multiple_of(w * CB, CB), CB)

    def block(side, k):
        return ob.at[side, pl.ds(pl.multiple_of(k * STEPS, STEPS), STEPS)]

    def window_send(side, k):
        return remote(block(side, k), st.at[side, :, :, lanes], s_1.at[side, k], r_1.at[side, w], (s, k, h))

    def window_keep(side):
        return pltpu.make_async_copy(block(side, w), st.at[side, :, :, lanes], s_1l.at[side])

    def own_window(k, carry):
        lax.fori_loop(k * 4, k * 4 + 4, own_steps, 0)

        @pl.when(k != w)
        def _():
            window_send(0, k).start()
            window_send(1, k).start()

        @pl.when(k == w)
        def _():
            window_keep(0).start()
            window_keep(1).start()

        return carry

    lax.fori_loop(0, TM, own_window, 0)

    def end_send(k):
        return remote(ubuf.at[k], wr.at[w], s_w.at[k], r_w.at[w], (s, k, h))

    def robin_send(side):
        return remote(
            st.at[side], robin_out.at[0, side], s_o.at[side], r_o.at[side],
            (left if side == 1 else right, w, h),
        )

    def finish_robin():
        for side in range(2):
            window_keep(side).wait()
            for d in range(1, TM):
                f = other(d)
                to = st.at[side, :, :, pl.ds(pl.multiple_of(f * CB, CB), CB)]
                remote(block(side, f), to, s_1.at[side, f], r_1.at[side, f], (s, f, h)).wait_recv()
            robin_send(side).start()

    def other_window(k, carry):
        remote(rb.at[oh, k], rb.at[oh, k], s_ro.at[k], r_rb.at[oh, k], (s, w, oh)).wait_recv()
        cross(k).wait_send()

        @pl.when(k < TM - 2)
        def _():
            cross(k + 2).start()

        @pl.when(k == TM - 1)
        def _():
            finish_robin()


        def body(bt, c):
            steps(k, oh, bt, False)
            return c

        lax.fori_loop(0, 4, body, 0)
        my_hi, my_lo = yi[h, 0], yi[h, 1]

        def y_inverse(g, c):
            a, b = pl.ds(g * 8, 4), pl.ds(g * 8 + 4, 4)
            rhs = jnp.concatenate(
                [modes[k + 1, :, a].reshape(256, CB), modes[k + 1, :, b].reshape(256, CB)], axis=1
            )
            res = const_dot(my_hi, my_lo, rhs)
            tbuf[:, a] = res[:, :CB].reshape(4, 4, 8, CB)
            tbuf[:, b] = res[:, CB:].reshape(4, 4, 8, CB)
            return c

        lax.fori_loop(0, 4, y_inverse, 0)

        def x_inverse(q, c):
            rhs = jnp.concatenate(
                [tbuf[2 * q].reshape(256, CB), tbuf[2 * q + 1].reshape(256, CB)], axis=1
            )
            res = const_dot(xi[0], xi[1], rhs)
            ubuf[k, 2 * q] = res[:, :CB].reshape(NX, 8, CB)
            ubuf[k, 2 * q + 1] = res[:, CB:].reshape(NX, 8, CB)
            return c

        lax.fori_loop(0, 2, x_inverse, 0)

        @pl.when(k != w)
        def _():
            end_send(k).start()

        return carry

    lax.fori_loop(0, TM, other_window, 0)

    def z_inverse(ref, index, b, first):
        def body(yt, c):
            hi, lo = split(ref[index, yt].reshape(NX * 8, CB))
            m_hi, m_lo = zi[0, b], zi[1, b]
            part = (dot(hi, m_hi) + (dot(lo, m_hi) + dot(hi, m_lo))).reshape(NX, 8, NZ)
            if first:
                acc[yt] = part
            else:
                acc[yt] += part
            return c

        lax.fori_loop(0, 4, body, 0)

    z_inverse(ubuf, w, w, True)
    for d in (1, 3, 2):
        f = other(d)
        remote(ubuf.at[f], wr.at[f], s_w.at[f], r_w.at[f], (s, f, h)).wait_recv()
        z_inverse(wr, f, f, False)

    def store(yt):
        rows = pl.ds(pl.multiple_of(yt * 8, 8), 8)
        return pltpu.make_async_copy(acc.at[yt], ends_out.at[0, :, rows, :], s_out.at[yt])

    for yt in range(4):
        store(yt).start()

    for c in small:
        c.wait_send()
    for c in same_half:
        c.wait_send()
    for d in range(1, TM):
        for side in range(2):
            window_send(side, other(d)).wait_send()
        end_send(other(d)).wait_send()
    for side in range(2):
        robin_send(side).wait()
    for yt in range(4):
        store(yt).wait()


def local(
    initial_state, heat_source, source_amplitude, diffusivity, robin_param,
    spectrum_x, spectrum_y, spectrum_z, robin_in, open_flag, owner_side,
):
    xf, yf, yi, xi, zf, zi = (jnp.asarray(c) for c in constants())
    hbm = pl.BlockSpec(memory_space=pltpu.HBM)
    dma = pltpu.SemaphoreType.DMA
    tile = (8, CB)
    return pl.pallas_call(
        sweep_kernel,
        out_shape=(
            jax.ShapeDtypeStruct((1, 2, STEPS, 32, NZ), F32),
            jax.ShapeDtypeStruct((1, NX, 32, NZ), F32),
        ),
        in_specs=[hbm] * 17,
        out_specs=(hbm, hbm),
        scratch_shapes=[
            pltpu.SMEM((STEPS,), F32), pltpu.SMEM((1,), F32), pltpu.SMEM((1,), F32),
            pltpu.SMEM((NX,), F32),
            pltpu.VMEM((1, 32), F32), pltpu.VMEM((1, NZ), F32),
            pltpu.VMEM((SPACE, 32), jnp.int32), pltpu.VMEM((SPACE, 32), jnp.int32),
            pltpu.VMEM(xf.shape, BF16), pltpu.VMEM(yf.shape, BF16), pltpu.VMEM(yi.shape, BF16),
            pltpu.VMEM(xi.shape, BF16), pltpu.VMEM(zi.shape, BF16),
            pltpu.VMEM((2, NX, 32, NZ), F32),
            pltpu.VMEM((NZ, 2 * CB), BF16),
            pltpu.VMEM((2, 4, 2, NX) + tile, F32),
            pltpu.VMEM((2, 32, CB), F32),
            pltpu.VMEM((3,) + tile, F32),
            pltpu.VMEM((TM, STEPS) + tile, F32),
            pltpu.VMEM((2, TM, 2, STEPS, 32, CB), F32),
            pltpu.VMEM((TM + 1, 8, NX) + tile, F32),
            pltpu.VMEM((8, NX) + tile, F32),
            pltpu.VMEM((8, NX) + tile, F32),
            pltpu.VMEM((STEPS, 4) + tile, F32),
            pltpu.VMEM((4, 32, CB), F32),
            pltpu.VMEM((2, TM * STEPS, 32, CB), F32),
            pltpu.VMEM((2, STEPS, 32, NZ), F32),
            pltpu.VMEM((4, NX) + tile, F32),
            pltpu.VMEM((TM, 4, NX) + tile, F32),
            pltpu.VMEM((TM, 4, NX) + tile, F32),
            pltpu.VMEM((4, NX, 8, NZ), F32),
            dma((13,)), dma((2, 4)), dma, dma, dma((TM,)), dma((2, TM)), dma((TM,)),
            dma((4,)), dma((4,)), dma, dma, dma((2,)), dma((2,)), dma((TM,)), dma((TM,)),
            dma((2, TM)), dma((2, TM)), dma((2,)), dma((2,)), dma((2,)),
            dma((TM,)), dma((TM,)), dma((4,)),
        ],
        compiler_params=pltpu.CompilerParams(
            collective_id=0, has_side_effects=True, vmem_limit_bytes=60 << 20
        ),
        name="sweep",
    )(
        initial_state, heat_source, robin_in, zf,
        source_amplitude, diffusivity, robin_param, spectrum_x,
        spectrum_y[None], spectrum_z[None], open_flag, owner_side,
        xf, yf, yi, xi, zi,
    )


def solution(mesh):
    placed = (
        P("space", "cores", None),
        P("space", "cores", None),
        P("tm"),
        P("space"),
        P("space"),
        P(),
        P("cores"),
        P(),
        P("space", None, "tm", "cores", None),
        P(None, "cores"),
        P(None, "cores"),
    )
    return jax.shard_map(
        local,
        mesh=mesh,
        in_specs=placed,
        out_specs=(P("space", None, "tm", "cores", None), P("tm", "space", "cores", None)),
        check_vma=False,
    )
```

```python
import functools

import jax
import jax.numpy as jnp
import ml_dtypes
import numpy as np
from jax import lax
from jax.experimental import pallas as pl
from jax.experimental.pallas import tpu as pltpu
from jax.sharding import PartitionSpec as P

MESH = pl.DeviceIdType.MESH
F32, BF16 = jnp.float32, jnp.bfloat16
NX, NY, NZ, STEPS, TM, SPACE = 32, 64, 512, 8, 4, 32
CB = NZ // TM
PERM = list(range(0, NX, 2)) + list(range(1, NX, 2))


def cosine(n):
    k = np.arange(n)[:, None]
    i = np.arange(n)[None, :]
    scale = np.where(k == 0, np.sqrt(1.0 / n), np.sqrt(2.0 / n))
    return scale * np.cos(np.pi * k * (i + 0.5) / n)


C_X, C_Y, C_Z = cosine(NX), cosine(NY), cosine(NZ)
EDGE = C_X[PERM, 0]
VALUE_W = [float(v) for v in EDGE * EDGE]
SLOPE_W = [float(v) for v in (C_X[PERM, 1] - C_X[PERM, 0]) * EDGE]


def split_constant(m):
    hi = np.asarray(m, np.float32).astype(ml_dtypes.bfloat16)
    lo = (np.asarray(m, np.float64) - hi.astype(np.float64)).astype(np.float32)
    return np.stack([hi, lo.astype(ml_dtypes.bfloat16)])


def constants():
    eye8, eye4 = np.eye(8), np.eye(4)
    x_fwd = np.kron(C_X[PERM] / EDGE[:, None], eye8)
    x_inv = np.kron((C_X[PERM] * EDGE[:, None]).T, eye8)
    cy = C_Y.reshape(8, 8, 8, 8)
    y_fwd = np.einsum("pbqy,ac->pabqcy", cy, eye4).reshape(256, 256)
    y_inv = np.einsum("pbqy,ac->qaypcb", cy, eye4).reshape(2, 128, 256)
    y_inv = np.stack([split_constant(y_inv[0]), split_constant(y_inv[1])])
    z_fwd = split_constant(C_Z.T)
    z_fwd = z_fwd.reshape(2, NZ, TM, CB).transpose(2, 1, 0, 3).reshape(TM, NZ, 2 * CB)
    z_inv = split_constant(C_Z).reshape(2, TM, CB, NZ)
    return (split_constant(x_fwd), split_constant(y_fwd), y_inv, split_constant(x_inv), z_fwd, z_inv)


def split(v):
    hi = v.astype(BF16)
    return hi, (v - hi.astype(F32)).astype(BF16)


def dot(a, b):
    return jnp.dot(a, b, preferred_element_type=F32)


def const_dot(m_hi, m_lo, v):
    hi, lo = split(v)
    return dot(m_hi, hi) + (dot(m_lo, hi) + dot(m_hi, lo))


def sweep_kernel(
    state_in, heat_in, robin_in, zf_in,
    amp_in, diff_in, param_in, specx_in, specy_in, specz_in, flag_in, owner_in,
    xf_in, yf_in, yi_in, xi_in, zi_in,
    robin_out, ends_out,
    amp_s, diff_s, param_s, specx_s, specy, specz, flag, owner,
    xf, yf, yi, xi, zi,
    xin, zf, v, sycol, ptile, amp, rb, modes, src, fac, tr, coef, ob, st, tbuf, ubuf, wr,
    s_c, s_in, s_zf, s_rl, s_rs, r_rb, s_ro, s_f, r_f, s_y, r_y, s_p, r_p, s_a, r_a,
    s_1, r_1, s_1l, s_o, r_o, s_w, r_w,
):
    s = lax.axis_index("space")
    w = lax.axis_index("tm")
    h = lax.axis_index("cores")
    oh = 1 - h
    left = lax.rem(s + SPACE - 1, SPACE)
    right = lax.rem(s + 1, SPACE)

    def remote(a, b, ss, rs, to):
        return pltpu.make_async_remote_copy(
            src_ref=a, dst_ref=b, send_sem=ss, recv_sem=rs, device_id=to, device_id_type=MESH
        )

    def other(d):
        return lax.rem(w + d, TM)

    barrier = pltpu.get_barrier_semaphore()
    for d in range(1, TM):
        pl.semaphore_signal(barrier, inc=1, device_id=(s, other(d), h), device_id_type=MESH)
    for to in ((s, w, oh), (left, w, h), (right, w, h)):
        pl.semaphore_signal(barrier, inc=1, device_id=to, device_id_type=MESH)

    ins = (state_in, heat_in)
    zf_copy = pltpu.make_async_copy(zf_in.at[w], zf, s_zf)
    zf_copy.start()
    operands = (
        (amp_in, amp_s), (param_in, param_s), (specy_in, specy), (xf_in, xf), (diff_in, diff_s),
        (specx_in, specx_s), (specz_in, specz), (flag_in, flag), (owner_in, owner),
        (yf_in, yf), (yi_in, yi), (xi_in, xi), (zi_in, zi),
    )
    loads = [pltpu.make_async_copy(a, b, s_c.at[i]) for i, (a, b) in enumerate(operands)]
    for c in loads[:4]:
        c.start()

    def load(i, yt):
        rows = pl.ds(pl.multiple_of(yt * 8, 8), 8)
        return pltpu.make_async_copy(ins[i].at[:, rows, :], xin.at[i, :, rows, :], s_in.at[i, yt])

    for yt in range(4):
        for i in range(2):
            load(i, yt).start()

    def robin_block(d):
        return robin_in.at[0, :, :, :, pl.ds(pl.multiple_of(d * CB, CB), CB)]

    own_robin = pltpu.make_async_copy(robin_block(w), rb.at[h, w], s_rl)
    own_robin.start()
    for c in loads[4:]:
        c.start()

    def column(row):
        n = row.shape[1]
        on = lax.broadcasted_iota(jnp.int32, (n, n), 0) == lax.broadcasted_iota(jnp.int32, (n, n), 1)
        picked = jnp.where(on, jnp.broadcast_to(row, (n, n)), 0.0)
        return jnp.broadcast_to(jnp.sum(picked, axis=1, keepdims=True), (n, CB))

    for c in loads[:3]:
        c.wait()
    for j in range(STEPS):
        amp[w, j] = jnp.full((8, CB), amp_s[j], F32)
    ptile[1] = jnp.full((8, CB), param_s[0], F32)
    sycol[h] = column(specy[...])
    def fwd_send(yt):
        return remote(v.at[h, yt], v.at[h, yt], s_f.at[yt], r_f.at[yt], (s, w, oh))

    zf_copy.wait()
    loads[3].wait()

    def transform(yt):
        rows = pl.ds(pl.multiple_of(yt * 8, 8), 8)
        zs = []
        for i in range(2):
            load(i, yt).wait()
            hi, lo = split(xin[i, :, rows, :].reshape(NX * 8, NZ))
            both = dot(hi, zf[...])
            zs.append(both[:, :CB] + (both[:, CB:] + dot(lo, zf[:, :CB])))
        res = const_dot(xf[0], xf[1], jnp.concatenate(zs, axis=1))
        v[h, yt, 0] = res[:, :CB].reshape(NX, 8, CB)
        v[h, yt, 1] = res[:, CB:].reshape(NX, 8, CB)

    transform(0)
    pl.semaphore_wait(barrier, 6)
    fwd_send(0).start()

    small = [
        remote(sycol.at[h], sycol.at[h], s_y, r_y, (s, w, oh)),
        remote(ptile.at[1], ptile.at[0], s_p.at[0], r_p.at[0], (right, w, h)),
        remote(ptile.at[1], ptile.at[2], s_p.at[1], r_p.at[1], (left, w, h)),
    ]
    for d in range(1, TM):
        small.append(remote(amp.at[w], amp.at[w], s_a.at[d], r_a.at[w], (s, other(d), h)))
    for c in small:
        c.start()
    same_half = []
    for d in range(1, TM):
        c = remote(robin_block(other(d)), rb.at[h, w], s_rs.at[d], r_rb.at[h, w], (s, other(d), h))
        c.start()
        same_half.append(c)

    def fwd_chunk(yt, carry):
        transform(yt)
        fwd_send(yt).start()
        return carry

    lax.fori_loop(1, 4, fwd_chunk, 0)

    for c in loads[4:9]:
        c.wait()
    remote(sycol.at[oh], sycol.at[oh], s_y, r_y, (s, w, oh)).wait_recv()
    small[1].wait_recv()
    small[2].wait_recv()

    def coefficient(at, here, beyond):
        opened = column(flag[pl.ds(at, 1), :].astype(F32))
        side = column(owner[pl.ds(at, 1), :].astype(F32))
        p = jnp.where(side > 0.5, beyond, here)
        return opened, opened * p

    pt = [jnp.broadcast_to(ptile[i][0:1], (32, CB)) for i in range(3)]
    o_l, op_l = coefficient(left, pt[0], pt[1])
    o_r, op_r = coefficient(s, pt[1], pt[2])
    coef[0] = o_l
    coef[1] = op_l
    coef[2] = o_r
    coef[3] = op_r

    sz = jnp.broadcast_to(specz[:, pl.ds(pl.multiple_of(w * CB, CB), CB)], (8, CB))

    def factor(bt, carry):
        sy = sycol[lax.div(bt, 4), pl.ds(pl.multiple_of(lax.rem(bt, 4) * 8, 8), 8), :]
        for a in range(NX):
            rate = (specx_s[PERM[a]] + sy) + sz
            fac[bt, a] = 1.0 / (1.0 + diff_s[0] * rate)
        return carry

    lax.fori_loop(0, 8, factor, 0)

    for yt in range(4):
        fwd_send(yt).wait_send()
    own_robin.wait()
    for d in range(1, TM):
        f = other(d)
        remote(rb.at[h, f], rb.at[h, f], s_rs.at[d], r_rb.at[h, f], (s, f, h)).wait_recv()
        remote(amp.at[f], amp.at[f], s_a.at[d], r_a.at[f], (s, f, h)).wait_recv()

    def cross(k):
        return remote(rb.at[h, k], rb.at[h, k], s_ro.at[k], r_rb.at[h, k], (s, w, oh))

    for k in range(2):
        cross(k).start()
    for c in loads[9:]:
        c.wait()

    for yt in range(4):
        remote(v.at[oh, yt], v.at[oh, yt], s_f.at[yt], r_f.at[yt], (s, w, oh)).wait_recv()

    def y_forward(g, carry):
        at = pl.ds(g * 4, 4)
        rhs = jnp.concatenate([v[:, :, i, at].reshape(256, CB) for i in range(2)], axis=1)
        res = const_dot(yf[0], yf[1], rhs)
        modes[0, :, at] = res[:, :CB].reshape(8, 4, 8, CB)
        src[:, at] = res[:, CB:].reshape(8, 4, 8, CB)
        return carry

    lax.fori_loop(0, 8, y_forward, 0)

    def steps(k, half, bt, traces):
        tile = half * 4 + bt
        rows = pl.ds(pl.multiple_of(bt * 8, 8), 8)
        for g in range(4):
            a0 = g * 8
            mu = [modes[k, tile, a0 + i] for i in range(8)]
            fs = [fac[tile, a0 + i] for i in range(8)]
            sg = [src[tile, a0 + i] for i in range(8)]
            for j in range(STEPS):
                r0 = rb[half, k, 0, j, rows, :]
                r1 = rb[half, k, 1, j, rows, :]
                p = r0 + r1 if g < 2 else r0 - r1
                am = amp[k, j]
                for i in range(8):
                    mu[i] = (mu[i] + (am * sg[i] + p)) * fs[i]
                if traces:
                    val = [VALUE_W[a0 + i] * mu[i] for i in range(8)]
                    slo = [SLOPE_W[a0 + i] * mu[i] for i in range(8)]
                    val = sum(val[1:], val[0])
                    slo = sum(slo[1:], slo[0])
                    if g % 2 == 0:
                        tr[j, g] = val
                        tr[j, g + 1] = slo
                    elif g == 1:
                        tr[j, 0] += val
                        tr[j, 1] += slo
                    else:
                        e0, e1 = tr[j, 0], tr[j, 1]
                        o0 = tr[j, 2] + val
                        o1 = tr[j, 3] + slo
                        at = k * STEPS + j
                        ob[1, at, rows, :] = coef[0, rows, :] * (e1 + o1) + coef[1, rows, :] * (e0 + o0)
                        ob[0, at, rows, :] = coef[3, rows, :] * (e0 - o0) - coef[2, rows, :] * (o1 - e1)
            for i in range(8):
                modes[k + 1, tile, a0 + i] = mu[i]

    def own_steps(t, carry):
        k, bt = lax.div(t, 4), lax.rem(t, 4)
        steps(k, h, bt, True)
        return carry

    lanes = pl.ds(pl.multiple_of(w * CB, CB), CB)

    def block(side, k):
        return ob.at[side, pl.ds(pl.multiple_of(k * STEPS, STEPS), STEPS)]

    def window_send(side, k):
        return remote(block(side, k), st.at[side, :, :, lanes], s_1.at[side, k], r_1.at[side, w], (s, k, h))

    def window_keep(side):
        return pltpu.make_async_copy(block(side, w), st.at[side, :, :, lanes], s_1l.at[side])

    def own_window(k, carry):
        lax.fori_loop(k * 4, k * 4 + 4, own_steps, 0)

        @pl.when(k != w)
        def _():
            window_send(0, k).start()
            window_send(1, k).start()

        @pl.when(k == w)
        def _():
            window_keep(0).start()
            window_keep(1).start()

        return carry

    lax.fori_loop(0, TM, own_window, 0)

    def end_send(k):
        return remote(ubuf.at[k], wr.at[w], s_w.at[k], r_w.at[w], (s, k, h))

    def robin_send(side):
        return remote(
            st.at[side], robin_out.at[0, side], s_o.at[side], r_o.at[side],
            (left if side == 1 else right, w, h),
        )

    def finish_robin():
        for side in range(2):
            window_keep(side).wait()
            for d in range(1, TM):
                f = other(d)
                to = st.at[side, :, :, pl.ds(pl.multiple_of(f * CB, CB), CB)]
                remote(block(side, f), to, s_1.at[side, f], r_1.at[side, f], (s, f, h)).wait_recv()
            robin_send(side).start()

    def other_window(k, carry):
        remote(rb.at[oh, k], rb.at[oh, k], s_ro.at[k], r_rb.at[oh, k], (s, w, oh)).wait_recv()
        cross(k).wait_send()

        @pl.when(k < TM - 2)
        def _():
            cross(k + 2).start()

        @pl.when(k == TM - 1)
        def _():
            finish_robin()


        def body(bt, c):
            steps(k, oh, bt, False)
            return c

        lax.fori_loop(0, 4, body, 0)
        my_hi, my_lo = yi[h, 0], yi[h, 1]

        def y_inverse(g, c):
            a, b = pl.ds(g * 8, 4), pl.ds(g * 8 + 4, 4)
            rhs = jnp.concatenate(
                [modes[k + 1, :, a].reshape(256, CB), modes[k + 1, :, b].reshape(256, CB)], axis=1
            )
            res = const_dot(my_hi, my_lo, rhs)
            tbuf[:, a] = res[:, :CB].reshape(4, 4, 8, CB)
            tbuf[:, b] = res[:, CB:].reshape(4, 4, 8, CB)
            return c

        lax.fori_loop(0, 4, y_inverse, 0)

        def x_inverse(q, c):
            rhs = jnp.concatenate(
                [tbuf[2 * q].reshape(256, CB), tbuf[2 * q + 1].reshape(256, CB)], axis=1
            )
            res = const_dot(xi[0], xi[1], rhs)
            ubuf[k, 2 * q] = res[:, :CB].reshape(NX, 8, CB)
            ubuf[k, 2 * q + 1] = res[:, CB:].reshape(NX, 8, CB)
            return c

        lax.fori_loop(0, 2, x_inverse, 0)

        @pl.when(k != w)
        def _():
            end_send(k).start()

        return carry

    lax.fori_loop(0, TM, other_window, 0)

    def z_inverse(ref, index, b, first):
        def body(yt, c):
            rows = pl.ds(pl.multiple_of(yt * 8, 8), 8)
            hi, lo = split(ref[index, yt].reshape(NX * 8, CB))
            m_hi, m_lo = zi[0, b], zi[1, b]
            part = (dot(hi, m_hi) + (dot(lo, m_hi) + dot(hi, m_lo))).reshape(NX, 8, NZ)
            if first:
                ends_out[0, :, rows, :] = part
            else:
                ends_out[0, :, rows, :] += part
            return c

        lax.fori_loop(0, 4, body, 0)

    z_inverse(ubuf, w, w, True)
    for d in (1, 3, 2):
        f = other(d)
        remote(ubuf.at[f], wr.at[f], s_w.at[f], r_w.at[f], (s, f, h)).wait_recv()
        z_inverse(wr, f, f, False)

    for c in small:
        c.wait_send()
    for c in same_half:
        c.wait_send()
    for d in range(1, TM):
        for side in range(2):
            window_send(side, other(d)).wait_send()
        end_send(other(d)).wait_send()
    for side in range(2):
        robin_send(side).wait()


def local(
    initial_state, heat_source, source_amplitude, diffusivity, robin_param,
    spectrum_x, spectrum_y, spectrum_z, robin_in, open_flag, owner_side,
):
    xf, yf, yi, xi, zf, zi = (jnp.asarray(c) for c in constants())
    hbm = pl.BlockSpec(memory_space=pltpu.HBM)
    dma = pltpu.SemaphoreType.DMA
    tile = (8, CB)
    return pl.pallas_call(
        sweep_kernel,
        out_shape=(
            pltpu.VMEM((1, 2, STEPS, 32, NZ), F32),
            pltpu.VMEM((1, NX, 32, NZ), F32),
        ),
        in_specs=[hbm] * 17,
        out_specs=(pl.BlockSpec(memory_space=pltpu.VMEM),) * 2,
        scratch_shapes=[
            pltpu.SMEM((STEPS,), F32), pltpu.SMEM((1,), F32), pltpu.SMEM((1,), F32),
            pltpu.SMEM((NX,), F32),
            pltpu.VMEM((1, 32), F32), pltpu.VMEM((1, NZ), F32),
            pltpu.VMEM((SPACE, 32), jnp.int32), pltpu.VMEM((SPACE, 32), jnp.int32),
            pltpu.VMEM(xf.shape, BF16), pltpu.VMEM(yf.shape, BF16), pltpu.VMEM(yi.shape, BF16),
            pltpu.VMEM(xi.shape, BF16), pltpu.VMEM(zi.shape, BF16),
            pltpu.VMEM((2, NX, 32, NZ), F32),
            pltpu.VMEM((NZ, 2 * CB), BF16),
            pltpu.VMEM((2, 4, 2, NX) + tile, F32),
            pltpu.VMEM((2, 32, CB), F32),
            pltpu.VMEM((3,) + tile, F32),
            pltpu.VMEM((TM, STEPS) + tile, F32),
            pltpu.VMEM((2, TM, 2, STEPS, 32, CB), F32),
            pltpu.VMEM((TM + 1, 8, NX) + tile, F32),
            pltpu.VMEM((8, NX) + tile, F32),
            pltpu.VMEM((8, NX) + tile, F32),
            pltpu.VMEM((STEPS, 4) + tile, F32),
            pltpu.VMEM((4, 32, CB), F32),
            pltpu.VMEM((2, TM * STEPS, 32, CB), F32),
            pltpu.VMEM((2, STEPS, 32, NZ), F32),
            pltpu.VMEM((4, NX) + tile, F32),
            pltpu.VMEM((TM, 4, NX) + tile, F32),
            pltpu.VMEM((TM, 4, NX) + tile, F32),
            dma((13,)), dma((2, 4)), dma, dma, dma((TM,)), dma((2, TM)), dma((TM,)),
            dma((4,)), dma((4,)), dma, dma, dma((2,)), dma((2,)), dma((TM,)), dma((TM,)),
            dma((2, TM)), dma((2, TM)), dma((2,)), dma((2,)), dma((2,)),
            dma((TM,)), dma((TM,)),
        ],
        compiler_params=pltpu.CompilerParams(
            collective_id=0, has_side_effects=True, vmem_limit_bytes=44 << 20
        ),
        name="sweep",
    )(*(v if v.size == 1 else pltpu.with_memory_space_constraint(v, pltpu.HBM) for v in (
        initial_state, heat_source, robin_in, zf,
        source_amplitude, diffusivity, robin_param, spectrum_x,
        spectrum_y[None], spectrum_z[None], open_flag, owner_side,
        xf, yf, yi, xi, zi,
    )))


def solution(mesh):
    placed = (
        P("space", "cores", None),
        P("space", "cores", None),
        P("tm"),
        P("space"),
        P("space"),
        P(),
        P("cores"),
        P(),
        P("space", None, "tm", "cores", None),
        P(None, "cores"),
        P(None, "cores"),
    )
    return jax.shard_map(
        local,
        mesh=mesh,
        in_specs=placed,
        out_specs=(P("space", None, "tm", "cores", None), P("tm", "space", "cores", None)),
        check_vma=False,
    )
```

```python
import functools

import jax
import jax.numpy as jnp
import ml_dtypes
import numpy as np
from jax import lax
from jax.experimental import pallas as pl
from jax.experimental.pallas import tpu as pltpu
from jax.sharding import PartitionSpec as P

MESH = pl.DeviceIdType.MESH
F32, BF16 = jnp.float32, jnp.bfloat16
NX, NY, NZ, STEPS, TM, SPACE = 32, 64, 512, 8, 4, 32
CB = NZ // TM
LANES = CB // 4
PERM = list(range(0, NX, 2)) + list(range(1, NX, 2))


def cosine(n):
    k = np.arange(n)[:, None]
    i = np.arange(n)[None, :]
    scale = np.where(k == 0, np.sqrt(1.0 / n), np.sqrt(2.0 / n))
    return scale * np.cos(np.pi * k * (i + 0.5) / n)


C_X, C_Y, C_Z = cosine(NX), cosine(NY), cosine(NZ)
EDGE = C_X[PERM, 0]
VALUE_W = [float(v) for v in EDGE * EDGE]
SLOPE_W = [float(v) for v in (C_X[PERM, 1] - C_X[PERM, 0]) * EDGE]


def split_constant(m):
    hi = np.asarray(m, np.float32).astype(ml_dtypes.bfloat16)
    lo = (np.asarray(m, np.float64) - hi.astype(np.float64)).astype(np.float32)
    return np.stack([hi, lo.astype(ml_dtypes.bfloat16)])


def constants():
    eye8, eye4 = np.eye(8), np.eye(4)
    x_fwd = np.kron(C_X[PERM] / EDGE[:, None], eye8)
    x_inv = np.kron((C_X[PERM] * EDGE[:, None]).T, eye8)
    cy = C_Y.reshape(8, 8, 8, 8)
    y_fwd = np.einsum("pbqy,ac->pabqcy", cy, eye4).reshape(256, 256)
    y_inv = np.einsum("pbqy,ac->qaypcb", cy, eye4).reshape(2, 128, 256)
    y_inv = np.stack([split_constant(y_inv[0]), split_constant(y_inv[1])])
    z_fwd = split_constant(C_Z.T)
    z_fwd = z_fwd.reshape(2, NZ, TM, CB).transpose(2, 1, 0, 3).reshape(TM, NZ, 2 * CB)
    z_inv = split_constant(C_Z).reshape(2, TM, 4, LANES, NZ).transpose(0, 2, 1, 3, 4).reshape(2, 4, CB, NZ)
    return (split_constant(x_fwd), split_constant(y_fwd), y_inv, split_constant(x_inv), z_fwd, z_inv)


def split(v):
    hi = v.astype(BF16)
    return hi, (v - hi.astype(F32)).astype(BF16)


def dot(a, b):
    return jnp.dot(a, b, preferred_element_type=F32)


def const_dot(m_hi, m_lo, v):
    hi, lo = split(v)
    return dot(m_hi, hi) + (dot(m_lo, hi) + dot(m_hi, lo))


def regroup(tiles):
    shape = tiles[0].shape
    t = [x.reshape(-1, CB) for x in tiles]
    lane = lax.broadcasted_iota(jnp.int32, t[0].shape, 1)
    low, even = lane < 64, lax.rem(lane, 64) < 32
    u = [None] * 4
    for a in (0, 1):
        u[a] = jnp.where(low, t[a], pltpu.roll(t[a + 2], 64, 1))
        u[a + 2] = jnp.where(low, pltpu.roll(t[a], 64, 1), t[a + 2])
    v = [None] * 4
    for a in (0, 2):
        v[a] = jnp.where(even, u[a], pltpu.roll(u[a + 1], 32, 1))
        v[a + 1] = jnp.where(even, pltpu.roll(u[a], 96, 1), u[a + 1])
    return [x.reshape(shape) for x in v]


def sweep_kernel(
    state_in, heat_in, robin_in, zf_in,
    amp_in, diff_in, param_in, specx_in, specy_in, specz_in, flag_in, owner_in,
    xf_in, yf_in, yi_in, xi_in, zi_in,
    robin_out, ends_out,
    amp_s, diff_s, param_s, specx_s, specy, specz, flag, owner,
    xf, yf, yi, xi, zi,
    xin, zf, v, sycol, ptile, amp, rin, rp, rb, modes, src, fac, tr, coef, ob, ob2, st,
    tbuf, xbuf, ubuf, wr,
    s_c, s_in, s_zf, s_rl, s_rs, r_rb, s_ro, r_ro, s_f, r_f, s_y, r_y, s_p, r_p, s_a, r_a,
    s_1, r_1, s_1l, s_o, r_o, s_w, r_w, s_wl,
):
    s = lax.axis_index("space")
    w = lax.axis_index("tm")
    h = lax.axis_index("cores")
    oh = 1 - h
    left = lax.rem(s + SPACE - 1, SPACE)
    right = lax.rem(s + 1, SPACE)

    def remote(a, b, ss, rs, to):
        return pltpu.make_async_remote_copy(
            src_ref=a, dst_ref=b, send_sem=ss, recv_sem=rs, device_id=to, device_id_type=MESH
        )

    def other(d):
        return lax.rem(w + d, TM)

    barrier = pltpu.get_barrier_semaphore()
    for d in range(1, TM):
        pl.semaphore_signal(barrier, inc=1, device_id=(s, other(d), h), device_id_type=MESH)
    for to in ((s, w, oh), (left, w, h), (right, w, h)):
        pl.semaphore_signal(barrier, inc=1, device_id=to, device_id_type=MESH)

    ins = (state_in, heat_in)
    zf_copy = pltpu.make_async_copy(zf_in.at[w], zf, s_zf)
    zf_copy.start()
    operands = (
        (amp_in, amp_s), (param_in, param_s), (specy_in, specy), (xf_in, xf), (diff_in, diff_s),
        (specx_in, specx_s), (specz_in, specz), (flag_in, flag), (owner_in, owner),
        (yf_in, yf), (yi_in, yi), (xi_in, xi), (zi_in, zi),
    )
    loads = [pltpu.make_async_copy(a, b, s_c.at[i]) for i, (a, b) in enumerate(operands)]
    for c in loads[:4]:
        c.start()

    def load(i, yt):
        rows = pl.ds(pl.multiple_of(yt * 8, 8), 8)
        return pltpu.make_async_copy(ins[i].at[:, rows, :], xin.at[i, :, rows, :], s_in.at[i, yt])

    for yt in range(4):
        for i in range(2):
            load(i, yt).start()

    own_robin = pltpu.make_async_copy(robin_in.at[0], rin, s_rl.at[0])
    own_robin.start()
    for c in loads[4:]:
        c.start()

    def column(row):
        n = row.shape[1]
        on = lax.broadcasted_iota(jnp.int32, (n, n), 0) == lax.broadcasted_iota(jnp.int32, (n, n), 1)
        picked = jnp.where(on, jnp.broadcast_to(row, (n, n)), 0.0)
        return jnp.broadcast_to(jnp.sum(picked, axis=1, keepdims=True), (n, CB))

    for c in loads[:3]:
        c.wait()
    for j in range(STEPS):
        amp[w, j] = jnp.full((8, CB), amp_s[j], F32)
    ptile[1] = jnp.full((8, CB), param_s[0], F32)
    sycol[h] = column(specy[...])
    def fwd_send(yt):
        return remote(v.at[h, yt], v.at[h, yt], s_f.at[yt], r_f.at[yt], (s, w, oh))

    zf_copy.wait()
    loads[3].wait()

    def transform(yt):
        rows = pl.ds(pl.multiple_of(yt * 8, 8), 8)
        zs = []
        for i in range(2):
            load(i, yt).wait()
            hi, lo = split(xin[i, :, rows, :].reshape(NX * 8, NZ))
            both = dot(hi, zf[...])
            zs.append(both[:, :CB] + (both[:, CB:] + dot(lo, zf[:, :CB])))
        res = const_dot(xf[0], xf[1], jnp.concatenate(zs, axis=1))
        v[h, yt, 0] = res[:, :CB].reshape(NX, 8, CB)
        v[h, yt, 1] = res[:, CB:].reshape(NX, 8, CB)

    transform(0)
    pl.semaphore_wait(barrier, 6)
    fwd_send(0).start()

    small = [
        remote(sycol.at[h], sycol.at[h], s_y, r_y, (s, w, oh)),
        remote(ptile.at[1], ptile.at[0], s_p.at[0], r_p.at[0], (right, w, h)),
        remote(ptile.at[1], ptile.at[2], s_p.at[1], r_p.at[1], (left, w, h)),
    ]
    for d in range(1, TM):
        small.append(remote(amp.at[w], amp.at[w], s_a.at[d], r_a.at[w], (s, other(d), h)))
    for c in small:
        c.start()
    own_robin.wait()

    def pack_robin(p, carry):
        lanes = pl.ds(pl.multiple_of(p * CB, CB), CB)
        for side in range(2):
            got = regroup([rin[side, :, pl.ds(8 * q, 8), lanes] for q in range(4)])
            for j in range(4):
                rp[p, j, side] = got[j]
        return carry

    lax.fori_loop(0, TM, pack_robin, 0)
    same_half = []
    for d in range(1, TM):
        c = remote(rp.at[other(d)], rb.at[h, :, w], s_rs.at[d], r_rb.at[w], (s, other(d), h))
        c.start()
        same_half.append(c)
    keep_robin = pltpu.make_async_copy(rp.at[w], rb.at[h, :, w], s_rl.at[1])
    keep_robin.start()

    def fwd_chunk(yt, carry):
        transform(yt)
        fwd_send(yt).start()
        return carry

    lax.fori_loop(1, 4, fwd_chunk, 0)

    for c in loads[4:9]:
        c.wait()
    remote(sycol.at[oh], sycol.at[oh], s_y, r_y, (s, w, oh)).wait_recv()
    small[1].wait_recv()
    small[2].wait_recv()

    def coefficient(at, here, beyond):
        opened = column(flag[pl.ds(at, 1), :].astype(F32))
        side = column(owner[pl.ds(at, 1), :].astype(F32))
        p = jnp.where(side > 0.5, beyond, here)
        return opened, opened * p

    pt = [jnp.broadcast_to(ptile[i][0:1], (32, CB)) for i in range(3)]
    o_l, op_l = coefficient(left, pt[0], pt[1])
    o_r, op_r = coefficient(s, pt[1], pt[2])
    for i, c in enumerate((o_l, op_l, o_r, op_r)):
        coef[i] = regroup([c[8 * q:8 * q + 8] for q in range(4)])[0]

    sz = jnp.broadcast_to(specz[:, pl.ds(pl.multiple_of(w * CB, CB), CB)], (8, CB))

    sz4 = regroup([sz] * 4)
    for half in range(2):
        sy = regroup([sycol[half, pl.ds(8 * q, 8), :] for q in range(4)])[0]

        def factor(a, carry):
            base = specx_s[a] + sy
            at = lax.div(a, 2) + lax.rem(a, 2) * (NX // 2)
            for j in range(4):
                fac[j, half, at] = 1.0 / (1.0 + diff_s[0] * (base + sz4[j]))
            return carry

        lax.fori_loop(0, NX, factor, 0)

    def clear(x, carry):
        ends_out[0, x] = jnp.zeros((32, NZ), F32)
        return carry

    lax.fori_loop(0, NX, clear, 0)

    for yt in range(4):
        fwd_send(yt).wait_send()
    keep_robin.wait()
    for d in range(1, TM):
        f = other(d)
        remote(rb.at[h, :, f], rb.at[h, :, f], s_rs.at[d], r_rb.at[f], (s, f, h)).wait_recv()
        remote(amp.at[f], amp.at[f], s_a.at[d], r_a.at[f], (s, f, h)).wait_recv()

    def cross(j):
        return remote(rb.at[h, j], rb.at[h, j], s_ro.at[j], r_ro.at[j], (s, w, oh))

    for j in range(2):
        cross(j).start()
    for c in loads[9:]:
        c.wait()

    for yt in range(4):
        remote(v.at[oh, yt], v.at[oh, yt], s_f.at[yt], r_f.at[yt], (s, w, oh)).wait_recv()

    def y_forward(g, carry):
        at = pl.ds(g * 4, 4)
        rhs = jnp.concatenate([v[:, :, i, at].reshape(256, CB) for i in range(2)], axis=1)
        res = const_dot(yf[0], yf[1], rhs)
        both = res.reshape(8, 4, 8, 2 * CB)
        for half in range(2):
            tiles = both[4 * half:4 * half + 4]
            got = regroup([tiles[q][:, :, :CB] for q in range(4)])
            for j in range(4):
                modes[0, j, half, at] = got[j]
            got = regroup([tiles[q][:, :, CB:] for q in range(4)])
            for j in range(4):
                src[j, half, at] = got[j]
        return carry

    lax.fori_loop(0, 8, y_forward, 0)

    def steps(k, half, j, traces):
        for g in range(4):
            a0 = g * 8
            mu = [modes[k, j, half, a0 + i] for i in range(8)]
            fs = [fac[j, half, a0 + i] for i in range(8)]
            sg = [src[j, half, a0 + i] for i in range(8)]
            for t in range(STEPS):
                r0 = rb[half, j, k, 0, t]
                r1 = rb[half, j, k, 1, t]
                p = r0 + r1 if g < 2 else r0 - r1
                am = amp[k, t]
                for i in range(8):
                    mu[i] = (mu[i] + (am * sg[i] + p)) * fs[i]
                if traces:
                    val = [VALUE_W[a0 + i] * mu[i] for i in range(8)]
                    slo = [SLOPE_W[a0 + i] * mu[i] for i in range(8)]
                    val = sum(val[1:], val[0])
                    slo = sum(slo[1:], slo[0])
                    if g % 2 == 0:
                        tr[t, g] = val
                        tr[t, g + 1] = slo
                    elif g == 1:
                        tr[t, 0] += val
                        tr[t, 1] += slo
                    else:
                        e0, e1 = tr[t, 0], tr[t, 1]
                        o0 = tr[t, 2] + val
                        o1 = tr[t, 3] + slo
                        ob[1, j, t] = coef[0] * (e1 + o1) + coef[1] * (e0 + o0)
                        ob[0, j, t] = coef[3] * (e0 - o0) - coef[2] * (o1 - e1)
            for i in range(8):
                modes[k + 1, j, half, a0 + i] = mu[i]

    lanes = pl.ds(pl.multiple_of(w * CB, CB), CB)

    def block(side, k):
        return ob2.at[side, k]

    def window_send(side, k):
        return remote(block(side, k), st.at[side, :, :, lanes], s_1.at[side, k], r_1.at[side, w], (s, k, h))

    def window_keep(side):
        return pltpu.make_async_copy(block(side, w), st.at[side, :, :, lanes], s_1l.at[side])

    def own_window(k, carry):
        def own_steps(j, c):
            steps(k, h, j, True)
            return c

        lax.fori_loop(0, 4, own_steps, 0)
        for side in range(2):
            got = regroup([ob[side, j] for j in range(4)])
            for q in range(4):
                ob2[side, k, :, pl.ds(8 * q, 8), :] = got[q]

        @pl.when(k != w)
        def _():
            window_send(0, k).start()
            window_send(1, k).start()

        @pl.when(k == w)
        def _():
            window_keep(0).start()
            window_keep(1).start()

        return carry

    lax.fori_loop(0, TM, own_window, 0)

    def end_send(j, k):
        return remote(ubuf.at[j, k], wr.at[j, w], s_w.at[j, k], r_w.at[j, w], (s, k, h))

    def end_keep(j):
        return pltpu.make_async_copy(ubuf.at[j, w], wr.at[j, w], s_wl.at[j])

    def robin_send(side):
        return remote(
            st.at[side], robin_out.at[0, side], s_o.at[side], r_o.at[side],
            (left if side == 1 else right, w, h),
        )

    def finish_robin():
        for side in range(2):
            window_keep(side).wait()
            for d in range(1, TM):
                f = other(d)
                to = st.at[side, :, :, pl.ds(pl.multiple_of(f * CB, CB), CB)]
                remote(block(side, f), to, s_1.at[side, f], r_1.at[side, f], (s, f, h)).wait_recv()
            robin_send(side).start()

    def quarter(j, carry):
        remote(rb.at[oh, j], rb.at[oh, j], s_ro.at[j], r_ro.at[j], (s, w, oh)).wait_recv()
        cross(j).wait_send()

        @pl.when(j < 2)
        def _():
            cross(j + 2).start()

        @pl.when(j == 3)
        def _():
            finish_robin()

        def body(k, c):
            steps(k, oh, j, False)
            return c

        lax.fori_loop(0, TM, body, 0)
        my_hi, my_lo = yi[h, 0], yi[h, 1]

        def y_inverse(g, c):
            at = pl.ds(pl.multiple_of(g * 8, 8), 8)
            tiles = []
            for half in range(2):
                tiles += regroup([modes[k + 1, j, half, at] for k in range(TM)])
            rhs = jnp.concatenate(
                [
                    jnp.concatenate([x[4 * i:4 * i + 4].reshape(32, CB) for x in tiles], axis=0)
                    for i in range(2)
                ],
                axis=1,
            )
            res = const_dot(my_hi, my_lo, rhs)
            tbuf[:, pl.ds(g * 8, 4)] = res[:, :CB].reshape(4, 4, 8, CB)
            tbuf[:, pl.ds(g * 8 + 4, 4)] = res[:, CB:].reshape(4, 4, 8, CB)
            return c

        lax.fori_loop(0, 4, y_inverse, 0)

        def x_inverse(q, c):
            rhs = jnp.concatenate(
                [tbuf[2 * q].reshape(256, CB), tbuf[2 * q + 1].reshape(256, CB)], axis=1
            )
            res = const_dot(xi[0], xi[1], rhs)
            xbuf[2 * q] = res[:, :CB].reshape(NX, 8, CB)
            xbuf[2 * q + 1] = res[:, CB:].reshape(NX, 8, CB)
            return c

        lax.fori_loop(0, 2, x_inverse, 0)

        def by_window(i, c):
            at = pl.ds(pl.multiple_of(i * 8, 8), 8)
            got = regroup([xbuf[yt, at] for yt in range(4)])
            for k in range(TM):
                ubuf[j, k, at] = got[k]
            return c

        lax.fori_loop(0, 4, by_window, 0)
        for d in range(1, TM):
            end_send(j, other(d)).start()
        end_keep(j).start()

        @pl.when(j > 0)
        def _():
            z_inverse(j - 1)

        return carry

    def z_inverse(j):
        end_keep(j).wait()
        for d in range(1, TM):
            f = other(d)
            remote(ubuf.at[j, f], wr.at[j, f], s_w.at[j, f], r_w.at[j, f], (s, f, h)).wait_recv()

        def body(i, c):
            at = pl.ds(pl.multiple_of(i * 8, 8), 8)
            got = regroup([wr[j, p, at] for p in range(TM)])
            hi, lo = split(jnp.concatenate([x.reshape(64, CB) for x in got], axis=0))
            m_hi, m_lo = zi[0, j], zi[1, j]
            part = dot(hi, m_hi) + (dot(lo, m_hi) + dot(hi, m_lo))
            for yt in range(4):
                ends_out[0, at, pl.ds(8 * yt, 8), :] += part[64 * yt:64 * yt + 64].reshape(8, 8, NZ)
            return c

        lax.fori_loop(0, 4, body, 0)

    lax.fori_loop(0, 4, quarter, 0)
    z_inverse(3)

    for c in small:
        c.wait_send()
    for c in same_half:
        c.wait_send()
    for d in range(1, TM):
        for side in range(2):
            window_send(side, other(d)).wait_send()
        for j in range(4):
            end_send(j, other(d)).wait_send()
    for side in range(2):
        robin_send(side).wait()


def local(
    initial_state, heat_source, source_amplitude, diffusivity, robin_param,
    spectrum_x, spectrum_y, spectrum_z, robin_in, open_flag, owner_side,
):
    xf, yf, yi, xi, zf, zi = (jnp.asarray(c) for c in constants())
    hbm = pl.BlockSpec(memory_space=pltpu.HBM)
    dma = pltpu.SemaphoreType.DMA
    tile = (8, CB)
    return pl.pallas_call(
        sweep_kernel,
        out_shape=(
            pltpu.VMEM((1, 2, STEPS, 32, NZ), F32),
            pltpu.VMEM((1, NX, 32, NZ), F32),
        ),
        in_specs=[hbm] * 17,
        out_specs=(pl.BlockSpec(memory_space=pltpu.VMEM),) * 2,
        scratch_shapes=[
            pltpu.SMEM((STEPS,), F32), pltpu.SMEM((1,), F32), pltpu.SMEM((1,), F32),
            pltpu.SMEM((NX,), F32),
            pltpu.VMEM((1, 32), F32), pltpu.VMEM((1, NZ), F32),
            pltpu.VMEM((SPACE, 32), jnp.int32), pltpu.VMEM((SPACE, 32), jnp.int32),
            pltpu.VMEM(xf.shape, BF16), pltpu.VMEM(yf.shape, BF16), pltpu.VMEM(yi.shape, BF16),
            pltpu.VMEM(xi.shape, BF16), pltpu.VMEM(zi.shape, BF16),
            pltpu.VMEM((2, NX, 32, NZ), F32),
            pltpu.VMEM((NZ, 2 * CB), BF16),
            pltpu.VMEM((2, 4, 2, NX) + tile, F32),
            pltpu.VMEM((2, 32, CB), F32),
            pltpu.VMEM((3,) + tile, F32),
            pltpu.VMEM((TM, STEPS) + tile, F32),
            pltpu.VMEM((2, STEPS, 32, NZ), F32),
            pltpu.VMEM((TM, 4, 2, STEPS) + tile, F32),
            pltpu.VMEM((2, 4, TM, 2, STEPS) + tile, F32),
            pltpu.VMEM((TM + 1, 4, 2, NX) + tile, F32),
            pltpu.VMEM((4, 2, NX) + tile, F32),
            pltpu.VMEM((4, 2, NX) + tile, F32),
            pltpu.VMEM((STEPS, 4) + tile, F32),
            pltpu.VMEM((4,) + tile, F32),
            pltpu.VMEM((2, 4, STEPS) + tile, F32),
            pltpu.VMEM((2, TM, STEPS, 32, CB), F32),
            pltpu.VMEM((2, STEPS, 32, NZ), F32),
            pltpu.VMEM((4, NX) + tile, F32),
            pltpu.VMEM((4, NX) + tile, F32),
            pltpu.VMEM((4, TM, NX) + tile, F32),
            pltpu.VMEM((4, TM, NX) + tile, F32),
            dma((13,)), dma((2, 4)), dma, dma((2,)), dma((TM,)), dma((TM,)), dma((4,)), dma((4,)),
            dma((4,)), dma((4,)), dma, dma, dma((2,)), dma((2,)), dma((TM,)), dma((TM,)),
            dma((2, TM)), dma((2, TM)), dma((2,)), dma((2,)), dma((2,)),
            dma((4, TM)), dma((4, TM)), dma((4,)),
        ],
        compiler_params=pltpu.CompilerParams(
            collective_id=0, has_side_effects=True, vmem_limit_bytes=44 << 20
        ),
        name="sweep",
    )(*(v if v.size == 1 else pltpu.with_memory_space_constraint(v, pltpu.HBM) for v in (
        initial_state, heat_source, robin_in, zf,
        source_amplitude, diffusivity, robin_param, spectrum_x,
        spectrum_y[None], spectrum_z[None], open_flag, owner_side,
        xf, yf, yi, xi, zi,
    )))


def solution(mesh):
    placed = (
        P("space", "cores", None),
        P("space", "cores", None),
        P("tm"),
        P("space"),
        P("space"),
        P(),
        P("cores"),
        P(),
        P("space", None, "tm", "cores", None),
        P(None, "cores"),
        P(None, "cores"),
    )
    return jax.shard_map(
        local,
        mesh=mesh,
        in_specs=placed,
        out_specs=(P("space", None, "tm", "cores", None), P("tm", "space", "cores", None)),
        check_vma=False,
    )
```

```python
import functools

import jax
import jax.numpy as jnp
import ml_dtypes
import numpy as np
from jax import lax
from jax.experimental import pallas as pl
from jax.experimental.pallas import tpu as pltpu
from jax.sharding import PartitionSpec as P

MESH = pl.DeviceIdType.MESH
F32, BF16 = jnp.float32, jnp.bfloat16
NX, NY, NZ, STEPS, TM, SPACE = 32, 64, 512, 8, 4, 32
CB = NZ // TM
LANES = CB // 4
PERM = list(range(0, NX, 2)) + list(range(1, NX, 2))


def cosine(n):
    k = np.arange(n)[:, None]
    i = np.arange(n)[None, :]
    scale = np.where(k == 0, np.sqrt(1.0 / n), np.sqrt(2.0 / n))
    return scale * np.cos(np.pi * k * (i + 0.5) / n)


C_X, C_Y, C_Z = cosine(NX), cosine(NY), cosine(NZ)
EDGE = C_X[PERM, 0]
VALUE_W = [float(v) for v in EDGE * EDGE]
SLOPE_W = [float(v) for v in (C_X[PERM, 1] - C_X[PERM, 0]) * EDGE]


def split_constant(m):
    hi = np.asarray(m, np.float32).astype(ml_dtypes.bfloat16)
    lo = (np.asarray(m, np.float64) - hi.astype(np.float64)).astype(np.float32)
    return np.stack([hi, lo.astype(ml_dtypes.bfloat16)])


def constants():
    eye8, eye4 = np.eye(8), np.eye(4)
    x_fwd = np.kron(C_X[PERM] / EDGE[:, None], eye8)
    x_inv = np.kron((C_X[PERM] * EDGE[:, None]).T, eye8)
    cy = C_Y.reshape(8, 8, 8, 8)
    y_fwd = np.einsum("pbqy,ac->pabqcy", cy, eye4).reshape(256, 256)
    y_inv = np.einsum("pbqy,ac->qaypcb", cy, eye4).reshape(2, 128, 256)
    y_inv = np.stack([split_constant(y_inv[0]), split_constant(y_inv[1])])
    z_fwd = split_constant(C_Z.T)
    z_fwd = z_fwd.reshape(2, NZ, TM, CB).transpose(2, 1, 0, 3).reshape(TM, NZ, 2 * CB)
    z_inv = split_constant(C_Z).reshape(2, TM, 4, LANES, NZ).transpose(0, 2, 1, 3, 4).reshape(2, 4, CB, NZ)
    z_inv = np.concatenate([z_inv[0], z_inv[0], z_inv[1]], axis=1)
    return (split_constant(x_fwd), split_constant(y_fwd), y_inv, split_constant(x_inv), z_fwd, z_inv)


def split(v):
    hi = v.astype(BF16)
    return hi, (v - hi.astype(F32)).astype(BF16)


def dot(a, b):
    return jnp.dot(a, b, preferred_element_type=F32)


def const_dot(m_hi, m_lo, v):
    hi, lo = split(v)
    return dot(m_hi, hi) + (dot(m_lo, hi) + dot(m_hi, lo))


def regroup(tiles):
    shape = tiles[0].shape
    t = [x.reshape(-1, CB) for x in tiles]
    lane = lax.broadcasted_iota(jnp.int32, t[0].shape, 1)
    low, even = lane < 64, lax.rem(lane, 64) < 32
    u = [None] * 4
    for a in (0, 1):
        u[a] = jnp.where(low, t[a], pltpu.roll(t[a + 2], 64, 1))
        u[a + 2] = jnp.where(low, pltpu.roll(t[a], 64, 1), t[a + 2])
    v = [None] * 4
    for a in (0, 2):
        v[a] = jnp.where(even, u[a], pltpu.roll(u[a + 1], 32, 1))
        v[a + 1] = jnp.where(even, pltpu.roll(u[a], 96, 1), u[a + 1])
    return [x.reshape(shape) for x in v]


def sweep_kernel(
    state_in, heat_in, robin_in, zf_in,
    amp_in, diff_in, param_in, specx_in, specy_in, specz_in, flag_in, owner_in,
    xf_in, yf_in, yi_in, xi_in, zi_in,
    robin_out, ends_out,
    amp_s, diff_s, param_s, specx_s, specy, specz, flag, owner,
    xf, yf, yi, xi, zi,
    xin, zf, vt, v, sycol, ptile, amp, rin, rp, rb, modes, src, fac, tr, coef, ob, st1, st,
    tbuf, xbuf, ubuf, wr,
    s_c, s_in, s_zf, s_rl, s_rs, r_rb, s_cw, r_cw, s_ro, r_ro, s_f, r_f, s_y, r_y, s_p, r_p, s_a, r_a,
    s_1, r_1, s_1l, s_o, r_o, s_w, r_w, s_wl,
):
    s = lax.axis_index("space")
    w = lax.axis_index("tm")
    h = lax.axis_index("cores")
    oh = 1 - h
    left = lax.rem(s + SPACE - 1, SPACE)
    right = lax.rem(s + 1, SPACE)

    def remote(a, b, ss, rs, to):
        return pltpu.make_async_remote_copy(
            src_ref=a, dst_ref=b, send_sem=ss, recv_sem=rs, device_id=to, device_id_type=MESH
        )

    def other(d):
        return lax.rem(w + d, TM)

    barrier = pltpu.get_barrier_semaphore()
    for d in range(1, TM):
        pl.semaphore_signal(barrier, inc=1, device_id=(s, other(d), h), device_id_type=MESH)
    for to in ((s, w, oh), (left, w, h), (right, w, h)):
        pl.semaphore_signal(barrier, inc=1, device_id=to, device_id_type=MESH)

    ins = (state_in, heat_in)
    own_robin = pltpu.make_async_copy(robin_in.at[0], rin, s_rl.at[0])
    own_robin.start()
    zf_copy = pltpu.make_async_copy(zf_in.at[w], zf, s_zf)
    zf_copy.start()
    operands = (
        (amp_in, amp_s), (param_in, param_s), (specy_in, specy), (xf_in, xf), (diff_in, diff_s),
        (specx_in, specx_s), (specz_in, specz), (flag_in, flag), (owner_in, owner),
        (yf_in, yf), (yi_in, yi), (xi_in, xi), (zi_in, zi),
    )
    loads = [pltpu.make_async_copy(a, b, s_c.at[i]) for i, (a, b) in enumerate(operands)]
    for c in loads[:4]:
        c.start()

    def load(i, yt):
        rows = pl.ds(pl.multiple_of(yt * 8, 8), 8)
        return pltpu.make_async_copy(ins[i].at[:, rows, :], xin.at[i, :, rows, :], s_in.at[i, yt])

    for yt in range(4):
        for i in range(2):
            load(i, yt).start()

    for c in loads[4:]:
        c.start()

    def column(row):
        n = row.shape[1]
        on = lax.broadcasted_iota(jnp.int32, (n, n), 0) == lax.broadcasted_iota(jnp.int32, (n, n), 1)
        picked = jnp.where(on, jnp.broadcast_to(row, (n, n)), 0.0)
        return jnp.broadcast_to(jnp.sum(picked, axis=1, keepdims=True), (n, CB))

    for c in loads[:3]:
        c.wait()
    for j in range(STEPS):
        amp[w, j] = jnp.full((8, CB), amp_s[j], F32)
    ptile[1] = jnp.full((8, CB), param_s[0], F32)
    sycol[h] = column(specy[...])
    own_robin.wait()

    def pack_robin(p, carry):
        lanes = pl.ds(pl.multiple_of(p * CB, CB), CB)
        for side in range(2):
            got = regroup([rin[side, :, pl.ds(8 * q, 8), lanes] for q in range(4)])
            for j in range(4):
                rp[p, j, side] = got[j]
        return carry

    pack_robin(w, 0)
    pl.semaphore_wait(barrier, 6)
    cross_own = remote(rp.at[w], rb.at[h, :, w], s_cw, r_cw, (s, w, oh))
    cross_own.start()
    keep_robin = pltpu.make_async_copy(rp.at[w], rb.at[h, :, w], s_rl.at[1])
    keep_robin.start()
    same_half = []
    for d in range(1, TM):
        pack_robin(other(d), 0)
        c = remote(rp.at[other(d)], rb.at[h, :, w], s_rs.at[d], r_rb.at[w], (s, other(d), h))
        c.start()
        same_half.append(c)

    def fwd_send(j):
        return remote(v.at[h, j], v.at[h, j], s_f.at[j], r_f.at[j], (s, w, oh))

    zf_copy.wait()
    loads[3].wait()

    def transform(yt, carry):
        rows = pl.ds(pl.multiple_of(yt * 8, 8), 8)
        zs = []
        for i in range(2):
            load(i, yt).wait()
            hi, lo = split(xin[i, :, rows, :].reshape(NX * 8, NZ))
            both = dot(hi, zf[...])
            zs.append(both[:, :CB] + (both[:, CB:] + dot(lo, zf[:, :CB])))
        res = const_dot(xf[0], xf[1], jnp.concatenate(zs, axis=1))
        vt[yt, 0] = res[:, :CB].reshape(NX, 8, CB)
        vt[yt, 1] = res[:, CB:].reshape(NX, 8, CB)
        return carry

    lax.fori_loop(0, 4, transform, 0)

    def pack_nodes(i, carry):
        at = pl.ds(pl.multiple_of(i * 8, 8), 8)
        for arr in range(2):
            got = regroup([vt[yt, arr, at] for yt in range(4)])
            for j in range(4):
                v[h, j, arr, at] = got[j]
        return carry

    lax.fori_loop(0, 4, pack_nodes, 0, unroll=True)
    for j in range(3):
        fwd_send(j).start()

    small = [
        remote(sycol.at[h], sycol.at[h], s_y, r_y, (s, w, oh)),
        remote(ptile.at[1], ptile.at[0], s_p.at[0], r_p.at[0], (right, w, h)),
        remote(ptile.at[1], ptile.at[2], s_p.at[1], r_p.at[1], (left, w, h)),
    ]
    for d in range(1, TM):
        small.append(remote(amp.at[w], amp.at[w], s_a.at[d], r_a.at[w], (s, other(d), h)))
    for c in small:
        c.start()

    for c in loads[4:9]:
        c.wait()
    remote(sycol.at[oh], sycol.at[oh], s_y, r_y, (s, w, oh)).wait_recv()
    small[1].wait_recv()
    small[2].wait_recv()

    def coefficient(at, here, beyond):
        opened = column(flag[pl.ds(at, 1), :].astype(F32))
        side = column(owner[pl.ds(at, 1), :].astype(F32))
        p = jnp.where(side > 0.5, beyond, here)
        return opened, opened * p

    pt = [jnp.broadcast_to(ptile[i][0:1], (32, CB)) for i in range(3)]
    o_l, op_l = coefficient(left, pt[0], pt[1])
    o_r, op_r = coefficient(s, pt[1], pt[2])
    for i, c in enumerate((o_l, op_l, o_r, op_r)):
        coef[i] = regroup([c[8 * q:8 * q + 8] for q in range(4)])[0]

    sz = jnp.broadcast_to(specz[:, pl.ds(pl.multiple_of(w * CB, CB), CB)], (8, CB))

    sz4 = regroup([sz] * 4)
    for half in range(2):
        sy = regroup([sycol[half, pl.ds(8 * q, 8), :] for q in range(4)])[0]

        def factor(a, carry):
            base = specx_s[a] + sy
            at = lax.div(a, 2) + lax.rem(a, 2) * (NX // 2)
            for j in range(4):
                fac[j, half, at] = 1.0 / (1.0 + diff_s[0] * (base + sz4[j]))
            return carry

        lax.fori_loop(0, NX, factor, 0)

    def clear(x, carry):
        ends_out[0, x] = jnp.zeros((32, NZ), F32)
        return carry

    lax.fori_loop(0, NX, clear, 0)

    keep_robin.wait()
    for d in range(1, TM):
        f = other(d)
        remote(rb.at[h, :, f], rb.at[h, :, f], s_rs.at[d], r_rb.at[f], (s, f, h)).wait_recv()
        remote(amp.at[f], amp.at[f], s_a.at[d], r_a.at[f], (s, f, h)).wait_recv()

    def cross(j, d):
        part = rb.at[h, j, other(d)]
        return remote(part, part, s_ro.at[j, d], r_ro.at[j, d], (s, w, oh))

    def cross_start(j):
        for d in range(1, TM):
            cross(j, d).start()

    for c in loads[9:]:
        c.wait()

    def y_forward(j):
        for i in range(2):
            def at(n):
                return pl.ds(16 * i + 4 * n, 4)

            sides = []
            for arr in range(2):
                rows = []
                for hh in range(2):
                    rows += regroup([v[hh, j, arr, at(n)] for n in range(4)])
                sides.append(jnp.concatenate([x.reshape(32, CB) for x in rows], axis=0))
            res = const_dot(yf[0], yf[1], jnp.concatenate(sides, axis=1))
            both = res.reshape(8, 4, 8, 2 * CB)
            for half in range(2):
                tiles = both[4 * half:4 * half + 4]
                got = regroup([tiles[q][:, :, :CB] for q in range(4)])
                for n in range(4):
                    modes[0, j, half, at(n)] = got[n]
                got = regroup([tiles[q][:, :, CB:] for q in range(4)])
                for n in range(4):
                    src[j, half, at(n)] = got[n]

    def steps(k, half, j, traces):
        for g in range(4):
            a0 = g * 8
            mu = [modes[k, j, half, a0 + i] for i in range(8)]
            fs = [fac[j, half, a0 + i] for i in range(8)]
            sg = [src[j, half, a0 + i] for i in range(8)]
            for t in range(STEPS):
                r0 = rb[half, j, k, 0, t]
                r1 = rb[half, j, k, 1, t]
                p = r0 + r1 if g < 2 else r0 - r1
                am = amp[k, t]
                for i in range(8):
                    mu[i] = (mu[i] + (am * sg[i] + p)) * fs[i]
                if traces:
                    val = [VALUE_W[a0 + i] * mu[i] for i in range(8)]
                    slo = [SLOPE_W[a0 + i] * mu[i] for i in range(8)]
                    val = sum(val[1:], val[0])
                    slo = sum(slo[1:], slo[0])
                    if g % 2 == 0:
                        tr[t, g] = val
                        tr[t, g + 1] = slo
                    elif g == 1:
                        tr[t, 0] += val
                        tr[t, 1] += slo
                    else:
                        e0, e1 = tr[t, 0], tr[t, 1]
                        o0 = tr[t, 2] + val
                        o1 = tr[t, 3] + slo
                        ob[k, j, 1, t] = coef[0] * (e1 + o1) + coef[1] * (e0 + o0)
                        ob[k, j, 0, t] = coef[3] * (e0 - o0) - coef[2] * (o1 - e1)
            for i in range(8):
                modes[k + 1, j, half, a0 + i] = mu[i]

    def window_send(j, k):
        return remote(ob.at[k, j], st1.at[w, j], s_1.at[j, k], r_1.at[j, w], (s, k, h))

    def window_keep(j):
        return pltpu.make_async_copy(ob.at[w, j], st1.at[w, j], s_1l.at[j])

    def own_quarter(j, carry):
        remote(v.at[oh, j], v.at[oh, j], s_f.at[j], r_f.at[j], (s, w, oh)).wait_recv()
        fwd_send(j).wait_send()

        @pl.when(j < 1)
        def _():
            fwd_send(j + 3).start()

        @pl.when(j >= 1)
        def _():
            cross_start(j - 1)

        y_forward(j)

        def own_steps(k, c):
            steps(k, h, j, True)
            return c

        lax.fori_loop(0, TM, own_steps, 0)
        for d in range(1, TM):
            window_send(j, other(d)).start()
        window_keep(j).start()
        return carry

    lax.fori_loop(0, 4, own_quarter, 0)

    def end_send(j, k):
        return remote(ubuf.at[j, k], wr.at[j, w], s_w.at[j, k], r_w.at[j, w], (s, k, h))

    def end_keep(j):
        return pltpu.make_async_copy(ubuf.at[j, w], wr.at[j, w], s_wl.at[j])

    def robin_send(side):
        return remote(
            st.at[side], robin_out.at[0, side], s_o.at[side], r_o.at[side],
            (left if side == 1 else right, w, h),
        )

    def unpack_robin():
        for j in range(4):
            window_keep(j).wait()
            for d in range(1, TM):
                f = other(d)
                remote(ob.at[f, j], st1.at[f, j], s_1.at[j, f], r_1.at[j, f], (s, f, h)).wait_recv()

        def unpack(p, c):
            lanes = pl.ds(pl.multiple_of(p * CB, CB), CB)
            for side in range(2):
                got = regroup([st1[p, j, side] for j in range(4)])
                for q in range(4):
                    st[side, :, pl.ds(8 * q, 8), lanes] = got[q]
            return c

        lax.fori_loop(0, TM, unpack, 0)

    def quarter(j, carry):
        for d in range(1, TM):
            part = rb.at[oh, j, other(d)]
            remote(part, part, s_ro.at[j, d], r_ro.at[j, d], (s, w, oh)).wait_recv()
            cross(j, d).wait_send()

        @pl.when(j == 0)
        def _():
            remote(rp.at[w], rb.at[oh, :, w], s_cw, r_cw, (s, w, oh)).wait_recv()

        @pl.when(j < 1)
        def _():
            cross_start(j + 3)

        @pl.when(j == 1)
        def _():
            unpack_robin()

        @pl.when(j == 3)
        def _():
            robin_send(0).start()
            robin_send(1).start()

        def body(k, c):
            steps(k, oh, j, False)
            return c

        lax.fori_loop(0, TM, body, 0)
        my_hi, my_lo = yi[h, 0], yi[h, 1]

        def y_inverse(g, c):
            at = pl.ds(pl.multiple_of(g * 8, 8), 8)
            tiles = []
            for half in range(2):
                tiles += regroup([modes[k + 1, j, half, at] for k in range(TM)])
            rhs = jnp.concatenate(
                [
                    jnp.concatenate([x[4 * i:4 * i + 4].reshape(32, CB) for x in tiles], axis=0)
                    for i in range(2)
                ],
                axis=1,
            )
            res = const_dot(my_hi, my_lo, rhs)
            tbuf[:, pl.ds(g * 8, 4)] = res[:, :CB].reshape(4, 4, 8, CB)
            tbuf[:, pl.ds(g * 8 + 4, 4)] = res[:, CB:].reshape(4, 4, 8, CB)
            return c

        lax.fori_loop(0, 4, y_inverse, 0, unroll=True)

        def x_inverse(q, c):
            rhs = jnp.concatenate(
                [tbuf[2 * q].reshape(256, CB), tbuf[2 * q + 1].reshape(256, CB)], axis=1
            )
            res = const_dot(xi[0], xi[1], rhs)
            xbuf[2 * q] = res[:, :CB].reshape(NX, 8, CB)
            xbuf[2 * q + 1] = res[:, CB:].reshape(NX, 8, CB)
            return c

        lax.fori_loop(0, 2, x_inverse, 0, unroll=True)

        def by_window(i, c):
            at = pl.ds(pl.multiple_of(i * 8, 8), 8)
            got = regroup([xbuf[yt, at] for yt in range(4)])
            for k in range(TM):
                ubuf[j, k, at] = got[k]
            return c

        lax.fori_loop(0, 4, by_window, 0, unroll=True)
        for d in range(1, TM):
            end_send(j, other(d)).start()
        end_keep(j).start()

        @pl.when(j > 0)
        def _():
            z_inverse(j - 1)

        return carry

    def z_inverse(j):
        end_keep(j).wait()
        for d in range(1, TM):
            f = other(d)
            remote(ubuf.at[j, f], wr.at[j, f], s_w.at[j, f], r_w.at[j, f], (s, f, h)).wait_recv()

        def body(i, c):
            at = pl.ds(pl.multiple_of(i * 8, 8), 8)
            got = regroup([wr[j, p, at] for p in range(TM)])
            hi, lo = split(jnp.concatenate([x.reshape(64, CB) for x in got], axis=0))
            part = dot(jnp.concatenate([hi, lo], axis=1), zi[j, :2 * CB]) + dot(hi, zi[j, 2 * CB:])
            for yt in range(4):
                ends_out[0, at, pl.ds(8 * yt, 8), :] += part[64 * yt:64 * yt + 64].reshape(8, 8, NZ)
            return c

        lax.fori_loop(0, 4, body, 0, unroll=True)

    lax.fori_loop(0, 4, quarter, 0)
    z_inverse(3)

    for c in small:
        c.wait_send()
    for c in same_half:
        c.wait_send()
    cross_own.wait_send()
    for d in range(1, TM):
        for j in range(4):
            window_send(j, other(d)).wait_send()
            end_send(j, other(d)).wait_send()
    for side in range(2):
        robin_send(side).wait()


def local(
    initial_state, heat_source, source_amplitude, diffusivity, robin_param,
    spectrum_x, spectrum_y, spectrum_z, robin_in, open_flag, owner_side,
):
    xf, yf, yi, xi, zf, zi = (jnp.asarray(c) for c in constants())
    hbm = pl.BlockSpec(memory_space=pltpu.HBM)
    dma = pltpu.SemaphoreType.DMA
    tile = (8, CB)
    return pl.pallas_call(
        sweep_kernel,
        out_shape=(
            pltpu.VMEM((1, 2, STEPS, 32, NZ), F32),
            pltpu.VMEM((1, NX, 32, NZ), F32),
        ),
        in_specs=[hbm] * 17,
        out_specs=(pl.BlockSpec(memory_space=pltpu.VMEM),) * 2,
        scratch_shapes=[
            pltpu.SMEM((STEPS,), F32), pltpu.SMEM((1,), F32), pltpu.SMEM((1,), F32),
            pltpu.SMEM((NX,), F32),
            pltpu.VMEM((1, 32), F32), pltpu.VMEM((1, NZ), F32),
            pltpu.VMEM((SPACE, 32), jnp.int32), pltpu.VMEM((SPACE, 32), jnp.int32),
            pltpu.VMEM(xf.shape, BF16), pltpu.VMEM(yf.shape, BF16), pltpu.VMEM(yi.shape, BF16),
            pltpu.VMEM(xi.shape, BF16), pltpu.VMEM(zi.shape, BF16),
            pltpu.VMEM((2, NX, 32, NZ), F32),
            pltpu.VMEM((NZ, 2 * CB), BF16),
            pltpu.VMEM((4, 2, NX) + tile, F32),
            pltpu.VMEM((2, 4, 2, NX) + tile, F32),
            pltpu.VMEM((2, 32, CB), F32),
            pltpu.VMEM((3,) + tile, F32),
            pltpu.VMEM((TM, STEPS) + tile, F32),
            pltpu.VMEM((2, STEPS, 32, NZ), F32),
            pltpu.VMEM((TM, 4, 2, STEPS) + tile, F32),
            pltpu.VMEM((2, 4, TM, 2, STEPS) + tile, F32),
            pltpu.VMEM((TM + 1, 4, 2, NX) + tile, F32),
            pltpu.VMEM((4, 2, NX) + tile, F32),
            pltpu.VMEM((4, 2, NX) + tile, F32),
            pltpu.VMEM((STEPS, 4) + tile, F32),
            pltpu.VMEM((4,) + tile, F32),
            pltpu.VMEM((TM, 4, 2, STEPS) + tile, F32),
            pltpu.VMEM((TM, 4, 2, STEPS) + tile, F32),
            pltpu.VMEM((2, STEPS, 32, NZ), F32),
            pltpu.VMEM((4, NX) + tile, F32),
            pltpu.VMEM((4, NX) + tile, F32),
            pltpu.VMEM((4, TM, NX) + tile, F32),
            pltpu.VMEM((4, TM, NX) + tile, F32),
            dma((13,)), dma((2, 4)), dma, dma((2,)), dma((TM,)), dma((TM,)), dma, dma,
            dma((4, TM)), dma((4, TM)),
            dma((4,)), dma((4,)), dma, dma, dma((2,)), dma((2,)), dma((TM,)), dma((TM,)),
            dma((4, TM)), dma((4, TM)), dma((4,)), dma((2,)), dma((2,)),
            dma((4, TM)), dma((4, TM)), dma((4,)),
        ],
        compiler_params=pltpu.CompilerParams(
            collective_id=0, has_side_effects=True, vmem_limit_bytes=44 << 20
        ),
        name="sweep",
    )(*(v if v.size == 1 else pltpu.with_memory_space_constraint(v, pltpu.HBM) for v in (
        initial_state, heat_source, robin_in, zf,
        source_amplitude, diffusivity, robin_param, spectrum_x,
        spectrum_y[None], spectrum_z[None], open_flag, owner_side,
        xf, yf, yi, xi, zi,
    )))


def solution(mesh):
    placed = (
        P("space", "cores", None),
        P("space", "cores", None),
        P("tm"),
        P("space"),
        P("space"),
        P(),
        P("cores"),
        P(),
        P("space", None, "tm", "cores", None),
        P(None, "cores"),
        P(None, "cores"),
    )
    return jax.shard_map(
        local,
        mesh=mesh,
        in_specs=placed,
        out_specs=(P("space", None, "tm", "cores", None), P("tm", "space", "cores", None)),
        check_vma=False,
    )
```

```python
import functools

import jax
import jax.numpy as jnp
import ml_dtypes
import numpy as np
from jax import lax
from jax.experimental import pallas as pl
from jax.experimental.pallas import tpu as pltpu
from jax.sharding import PartitionSpec as P

MESH = pl.DeviceIdType.MESH
F32, BF16 = jnp.float32, jnp.bfloat16
NX, NY, NZ, STEPS, TM, SPACE = 32, 64, 512, 8, 4, 32
CB = NZ // TM
LANES = CB // 4
PERM = list(range(0, NX, 2)) + list(range(1, NX, 2))


def cosine(n):
    k = np.arange(n)[:, None]
    i = np.arange(n)[None, :]
    scale = np.where(k == 0, np.sqrt(1.0 / n), np.sqrt(2.0 / n))
    return scale * np.cos(np.pi * k * (i + 0.5) / n)


C_X, C_Y, C_Z = cosine(NX), cosine(NY), cosine(NZ)
EDGE = C_X[PERM, 0]
VALUE_W = [float(v) for v in EDGE * EDGE]
SLOPE_W = [float(v) for v in (C_X[PERM, 1] - C_X[PERM, 0]) * EDGE]


def split_constant(m):
    hi = np.asarray(m, np.float32).astype(ml_dtypes.bfloat16)
    lo = (np.asarray(m, np.float64) - hi.astype(np.float64)).astype(np.float32)
    return np.stack([hi, lo.astype(ml_dtypes.bfloat16)])


def constants():
    eye8, eye4 = np.eye(8), np.eye(4)
    x_fwd = np.kron(C_X[PERM] / EDGE[:, None], eye8)
    x_inv = np.kron((C_X[PERM] * EDGE[:, None]).T, eye8)
    cy = C_Y.reshape(8, 8, 8, 8)
    y_fwd = np.einsum("pbqy,ac->pabqcy", cy, eye4).reshape(256, 256)
    y_inv = np.einsum("pbqy,ac->qaypcb", cy, eye4).reshape(2, 128, 256)
    y_inv = np.stack([split_constant(y_inv[0]), split_constant(y_inv[1])])
    z_fwd = split_constant(C_Z.T)
    z_fwd = z_fwd.reshape(2, NZ, TM, CB).transpose(2, 1, 0, 3).reshape(TM, NZ, 2 * CB)
    z_inv = split_constant(C_Z).reshape(2, TM, 4, LANES, NZ).transpose(0, 2, 1, 3, 4).reshape(2, 4, CB, NZ)
    z_inv = np.concatenate([z_inv[0], z_inv[0], z_inv[1]], axis=1)
    return (split_constant(x_fwd), split_constant(y_fwd), y_inv, split_constant(x_inv), z_fwd, z_inv)


def split(v):
    hi = v.astype(BF16)
    return hi, (v - hi.astype(F32)).astype(BF16)


def dot(a, b):
    return jnp.dot(a, b, preferred_element_type=F32)


def const_dot(m_hi, m_lo, v):
    hi, lo = split(v)
    return dot(m_hi, hi) + (dot(m_lo, hi) + dot(m_hi, lo))


def regroup(tiles):
    shape = tiles[0].shape
    t = [x.reshape(-1, CB) for x in tiles]
    lane = lax.broadcasted_iota(jnp.int32, t[0].shape, 1)
    low, even = lane < 64, lax.rem(lane, 64) < 32
    u = [None] * 4
    for a in (0, 1):
        u[a] = jnp.where(low, t[a], pltpu.roll(t[a + 2], 64, 1))
        u[a + 2] = jnp.where(low, pltpu.roll(t[a], 64, 1), t[a + 2])
    v = [None] * 4
    for a in (0, 2):
        v[a] = jnp.where(even, u[a], pltpu.roll(u[a + 1], 32, 1))
        v[a + 1] = jnp.where(even, pltpu.roll(u[a], 96, 1), u[a + 1])
    return [x.reshape(shape) for x in v]


def sweep_kernel(
    state_in, heat_in, robin_in, zf_in,
    amp_in, diff_in, param_in, specx_in, specy_in, specz_in, flag_in, owner_in,
    xf_in, yf_in, yi_in, xi_in, zi_in,
    robin_out, ends_out,
    amp_s, diff_s, param_s, specx_s, specy, specz, flag, owner,
    xf, yf, yi, xi, zi,
    xin, zf, vt, v, sycol, ptile, amp, rin, rp, rb, modes, src, fac, tr, coef, ob, st1, st,
    tbuf, xbuf, ubuf, wr,
    s_c, s_in, s_zf, s_rl, s_rs, r_rb, s_cw, r_cw, s_ro, r_ro, s_f, r_f, s_y, r_y, s_p, r_p, s_a, r_a,
    s_1, r_1, s_1l, s_o, r_o, s_w, r_w, s_wl,
):
    s = lax.axis_index("space")
    w = lax.axis_index("tm")
    h = lax.axis_index("cores")
    oh = 1 - h
    left = lax.rem(s + SPACE - 1, SPACE)
    right = lax.rem(s + 1, SPACE)

    def remote(a, b, ss, rs, to):
        return pltpu.make_async_remote_copy(
            src_ref=a, dst_ref=b, send_sem=ss, recv_sem=rs, device_id=to, device_id_type=MESH
        )

    def other(d):
        return lax.rem(w + d, TM)

    barrier = pltpu.get_barrier_semaphore()
    for d in range(1, TM):
        pl.semaphore_signal(barrier, inc=1, device_id=(s, other(d), h), device_id_type=MESH)
    for to in ((s, w, oh), (left, w, h), (right, w, h)):
        pl.semaphore_signal(barrier, inc=1, device_id=to, device_id_type=MESH)

    ins = (state_in, heat_in)
    own_robin = pltpu.make_async_copy(robin_in.at[0], rin, s_rl.at[0])
    own_robin.start()
    zf_copy = pltpu.make_async_copy(zf_in.at[w], zf, s_zf)
    zf_copy.start()
    operands = (
        (amp_in, amp_s), (param_in, param_s), (specy_in, specy), (xf_in, xf), (diff_in, diff_s),
        (specx_in, specx_s), (specz_in, specz), (flag_in, flag), (owner_in, owner),
        (yf_in, yf), (yi_in, yi), (xi_in, xi), (zi_in, zi),
    )
    loads = [pltpu.make_async_copy(a, b, s_c.at[i]) for i, (a, b) in enumerate(operands)]
    for c in loads[:4]:
        c.start()

    def load(i, yt):
        rows = pl.ds(pl.multiple_of(yt * 8, 8), 8)
        return pltpu.make_async_copy(ins[i].at[:, rows, :], xin.at[i, :, rows, :], s_in.at[i, yt])

    for yt in range(4):
        for i in range(2):
            load(i, yt).start()

    for c in loads[4:]:
        c.start()

    def column(row):
        n = row.shape[1]
        on = lax.broadcasted_iota(jnp.int32, (n, n), 0) == lax.broadcasted_iota(jnp.int32, (n, n), 1)
        picked = jnp.where(on, jnp.broadcast_to(row, (n, n)), 0.0)
        return jnp.broadcast_to(jnp.sum(picked, axis=1, keepdims=True), (n, CB))

    for c in loads[:3]:
        c.wait()
    for j in range(STEPS):
        amp[w, j] = jnp.full((8, CB), amp_s[j], F32)
    ptile[1] = jnp.full((8, CB), param_s[0], F32)
    sycol[h] = column(specy[...])
    own_robin.wait()

    def pack_robin(p, carry):
        lanes = pl.ds(pl.multiple_of(p * CB, CB), CB)
        for side in range(2):
            got = regroup([rin[side, :, pl.ds(8 * q, 8), lanes] for q in range(4)])
            for j in range(4):
                rp[p, j, side] = got[j]
        return carry

    pack_robin(w, 0)
    pl.semaphore_wait(barrier, 6)
    cross_own = remote(rp.at[w], rb.at[h, :, w], s_cw, r_cw, (s, w, oh))
    cross_own.start()
    keep_robin = pltpu.make_async_copy(rp.at[w], rb.at[h, :, w], s_rl.at[1])
    keep_robin.start()
    same_half = []
    for d in range(1, TM):
        pack_robin(other(d), 0)
        c = remote(rp.at[other(d)], rb.at[h, :, w], s_rs.at[d], r_rb.at[w], (s, other(d), h))
        c.start()
        same_half.append(c)

    def fwd_send(j):
        return remote(v.at[h, j], v.at[h, j], s_f.at[j], r_f.at[j], (s, w, oh))

    zf_copy.wait()
    loads[3].wait()

    def transform(yt, carry):
        rows = pl.ds(pl.multiple_of(yt * 8, 8), 8)
        zs = []
        for i in range(2):
            load(i, yt).wait()
            hi, lo = split(xin[i, :, rows, :].reshape(NX * 8, NZ))
            both = dot(hi, zf[...])
            zs.append(both[:, :CB] + (both[:, CB:] + dot(lo, zf[:, :CB])))
        res = const_dot(xf[0], xf[1], jnp.concatenate(zs, axis=1))
        vt[yt, 0] = res[:, :CB].reshape(NX, 8, CB)
        vt[yt, 1] = res[:, CB:].reshape(NX, 8, CB)
        return carry

    lax.fori_loop(0, 4, transform, 0, unroll=True)

    def pack_nodes(i, carry):
        at = pl.ds(pl.multiple_of(i * 8, 8), 8)
        for arr in range(2):
            got = regroup([vt[yt, arr, at] for yt in range(4)])
            for j in range(4):
                v[h, j, arr, at] = got[j]
        return carry

    lax.fori_loop(0, 4, pack_nodes, 0, unroll=True)
    for j in range(3):
        fwd_send(j).start()

    small = [
        remote(sycol.at[h], sycol.at[h], s_y, r_y, (s, w, oh)),
        remote(ptile.at[1], ptile.at[0], s_p.at[0], r_p.at[0], (right, w, h)),
        remote(ptile.at[1], ptile.at[2], s_p.at[1], r_p.at[1], (left, w, h)),
    ]
    for d in range(1, TM):
        small.append(remote(amp.at[w], amp.at[w], s_a.at[d], r_a.at[w], (s, other(d), h)))
    for c in small:
        c.start()

    for c in loads[4:9]:
        c.wait()
    remote(sycol.at[oh], sycol.at[oh], s_y, r_y, (s, w, oh)).wait_recv()
    small[1].wait_recv()
    small[2].wait_recv()

    def coefficient(at, here, beyond):
        opened = column(flag[pl.ds(at, 1), :].astype(F32))
        side = column(owner[pl.ds(at, 1), :].astype(F32))
        p = jnp.where(side > 0.5, beyond, here)
        return opened, opened * p

    pt = [jnp.broadcast_to(ptile[i][0:1], (32, CB)) for i in range(3)]
    o_l, op_l = coefficient(left, pt[0], pt[1])
    o_r, op_r = coefficient(s, pt[1], pt[2])
    for i, c in enumerate((o_l, op_l, o_r, op_r)):
        coef[i] = regroup([c[8 * q:8 * q + 8] for q in range(4)])[0]

    sz = jnp.broadcast_to(specz[:, pl.ds(pl.multiple_of(w * CB, CB), CB)], (8, CB))

    sz4 = regroup([sz] * 4)
    for half in range(2):
        sy = regroup([sycol[half, pl.ds(8 * q, 8), :] for q in range(4)])[0]

        def factor(a, carry):
            base = specx_s[a] + sy
            at = lax.div(a, 2) + lax.rem(a, 2) * (NX // 2)
            for j in range(4):
                fac[j, half, at] = 1.0 / (1.0 + diff_s[0] * (base + sz4[j]))
            return carry

        lax.fori_loop(0, NX, factor, 0)

    def clear(x, carry):
        ends_out[0, x] = jnp.zeros((32, NZ), F32)
        return carry

    lax.fori_loop(0, NX, clear, 0)

    keep_robin.wait()
    for d in range(1, TM):
        f = other(d)
        remote(rb.at[h, :, f], rb.at[h, :, f], s_rs.at[d], r_rb.at[f], (s, f, h)).wait_recv()
        remote(amp.at[f], amp.at[f], s_a.at[d], r_a.at[f], (s, f, h)).wait_recv()

    def cross(j, d):
        part = rb.at[h, j, other(d)]
        return remote(part, part, s_ro.at[j, d], r_ro.at[j, d], (s, w, oh))

    def cross_start(j):
        for d in range(1, TM):
            cross(j, d).start()

    for c in loads[9:]:
        c.wait()

    def y_forward(j):
        for i in range(2):
            def at(n):
                return pl.ds(16 * i + 4 * n, 4)

            sides = []
            for arr in range(2):
                rows = []
                for hh in range(2):
                    rows += regroup([v[hh, j, arr, at(n)] for n in range(4)])
                sides.append(jnp.concatenate([x.reshape(32, CB) for x in rows], axis=0))
            res = const_dot(yf[0], yf[1], jnp.concatenate(sides, axis=1))
            both = res.reshape(8, 4, 8, 2 * CB)
            for half in range(2):
                tiles = both[4 * half:4 * half + 4]
                got = regroup([tiles[q][:, :, :CB] for q in range(4)])
                for n in range(4):
                    modes[0, j, half, at(n)] = got[n]
                got = regroup([tiles[q][:, :, CB:] for q in range(4)])
                for n in range(4):
                    src[j, half, at(n)] = got[n]

    def steps(k, half, j, traces):
        for g in range(4):
            a0 = g * 8
            mu = [modes[k, j, half, a0 + i] for i in range(8)]
            fs = [fac[j, half, a0 + i] for i in range(8)]
            sg = [src[j, half, a0 + i] for i in range(8)]
            for t in range(STEPS):
                r0 = rb[half, j, k, 0, t]
                r1 = rb[half, j, k, 1, t]
                p = r0 + r1 if g < 2 else r0 - r1
                am = amp[k, t]
                for i in range(8):
                    mu[i] = (mu[i] + (am * sg[i] + p)) * fs[i]
                if traces:
                    val = [VALUE_W[a0 + i] * mu[i] for i in range(8)]
                    slo = [SLOPE_W[a0 + i] * mu[i] for i in range(8)]
                    val = sum(val[1:], val[0])
                    slo = sum(slo[1:], slo[0])
                    if g % 2 == 0:
                        tr[t, g] = val
                        tr[t, g + 1] = slo
                    elif g == 1:
                        tr[t, 0] += val
                        tr[t, 1] += slo
                    else:
                        e0, e1 = tr[t, 0], tr[t, 1]
                        o0 = tr[t, 2] + val
                        o1 = tr[t, 3] + slo
                        ob[k, j, 1, t] = coef[0] * (e1 + o1) + coef[1] * (e0 + o0)
                        ob[k, j, 0, t] = coef[3] * (e0 - o0) - coef[2] * (o1 - e1)
            for i in range(8):
                modes[k + 1, j, half, a0 + i] = mu[i]

    def window_send(j, k):
        return remote(ob.at[k, j], st1.at[w, j], s_1.at[j, k], r_1.at[j, w], (s, k, h))

    def window_keep(j):
        return pltpu.make_async_copy(ob.at[w, j], st1.at[w, j], s_1l.at[j])

    def own_quarter(j, carry):
        remote(v.at[oh, j], v.at[oh, j], s_f.at[j], r_f.at[j], (s, w, oh)).wait_recv()
        fwd_send(j).wait_send()

        @pl.when(j < 1)
        def _():
            fwd_send(j + 3).start()

        @pl.when(j >= 1)
        def _():
            cross_start(j - 1)

        y_forward(j)

        def own_steps(k, c):
            steps(k, h, j, True)
            return c

        lax.fori_loop(0, TM, own_steps, 0)
        for d in range(1, TM):
            window_send(j, other(d)).start()
        window_keep(j).start()
        return carry

    lax.fori_loop(0, 4, own_quarter, 0)

    def end_send(j, k):
        return remote(ubuf.at[j, k], wr.at[j, w], s_w.at[j, k], r_w.at[j, w], (s, k, h))

    def end_keep(j):
        return pltpu.make_async_copy(ubuf.at[j, w], wr.at[j, w], s_wl.at[j])

    def robin_send(side):
        return remote(
            st.at[side], robin_out.at[0, side], s_o.at[side], r_o.at[side],
            (jnp.where(side == 1, left, right), w, h),
        )

    def unpack_robin():
        for j in range(4):
            window_keep(j).wait()
            for d in range(1, TM):
                f = other(d)
                remote(ob.at[f, j], st1.at[f, j], s_1.at[j, f], r_1.at[j, f], (s, f, h)).wait_recv()

        def unpack(p, c):
            lanes = pl.ds(pl.multiple_of(p * CB, CB), CB)
            for side in range(2):
                got = regroup([st1[p, j, side] for j in range(4)])
                for q in range(4):
                    st[side, :, pl.ds(8 * q, 8), lanes] = got[q]
            return c

        lax.fori_loop(0, TM, unpack, 0)

    def quarter(j, carry):
        for d in range(1, TM):
            part = rb.at[oh, j, other(d)]
            remote(part, part, s_ro.at[j, d], r_ro.at[j, d], (s, w, oh)).wait_recv()
            cross(j, d).wait_send()

        @pl.when(j == 0)
        def _():
            remote(rp.at[w], rb.at[oh, :, w], s_cw, r_cw, (s, w, oh)).wait_recv()

        @pl.when(j < 1)
        def _():
            cross_start(j + 3)

        @pl.when(j == 1)
        def _():
            unpack_robin()

        @pl.when(j >= 2)
        def _():
            robin_send(j - 2).start()

        def body(k, c):
            steps(k, oh, j, False)
            return c

        lax.fori_loop(0, TM, body, 0)
        my_hi, my_lo = yi[h, 0], yi[h, 1]

        def y_inverse(g, c):
            at = pl.ds(pl.multiple_of(g * 8, 8), 8)
            tiles = []
            for half in range(2):
                tiles += regroup([modes[k + 1, j, half, at] for k in range(TM)])
            rhs = jnp.concatenate(
                [
                    jnp.concatenate([x[4 * i:4 * i + 4].reshape(32, CB) for x in tiles], axis=0)
                    for i in range(2)
                ],
                axis=1,
            )
            res = const_dot(my_hi, my_lo, rhs)
            tbuf[:, pl.ds(g * 8, 4)] = res[:, :CB].reshape(4, 4, 8, CB)
            tbuf[:, pl.ds(g * 8 + 4, 4)] = res[:, CB:].reshape(4, 4, 8, CB)
            return c

        lax.fori_loop(0, 4, y_inverse, 0, unroll=True)

        def x_inverse(q, c):
            rhs = jnp.concatenate(
                [tbuf[2 * q].reshape(256, CB), tbuf[2 * q + 1].reshape(256, CB)], axis=1
            )
            res = const_dot(xi[0], xi[1], rhs)
            xbuf[2 * q] = res[:, :CB].reshape(NX, 8, CB)
            xbuf[2 * q + 1] = res[:, CB:].reshape(NX, 8, CB)
            return c

        lax.fori_loop(0, 2, x_inverse, 0, unroll=True)

        def by_window(i, c):
            at = pl.ds(pl.multiple_of(i * 8, 8), 8)
            got = regroup([xbuf[yt, at] for yt in range(4)])
            for k in range(TM):
                ubuf[j, k, at] = got[k]
            return c

        lax.fori_loop(0, 4, by_window, 0, unroll=True)
        for d in range(1, TM):
            end_send(j, other(d)).start()
        end_keep(j).start()

        @pl.when(j > 1)
        def _():
            z_inverse(j - 2, 0)

        return carry

    def z_inverse(j, carry):
        end_keep(j).wait()
        for d in range(1, TM):
            f = other(d)
            remote(ubuf.at[j, f], wr.at[j, f], s_w.at[j, f], r_w.at[j, f], (s, f, h)).wait_recv()

        def body(i, c):
            at = pl.ds(pl.multiple_of(i * 8, 8), 8)
            got = regroup([wr[j, p, at] for p in range(TM)])
            hi, lo = split(jnp.concatenate([x.reshape(64, CB) for x in got], axis=0))
            part = dot(jnp.concatenate([hi, lo], axis=1), zi[j, :2 * CB]) + dot(hi, zi[j, 2 * CB:])
            for yt in range(4):
                ends_out[0, at, pl.ds(8 * yt, 8), :] += part[64 * yt:64 * yt + 64].reshape(8, 8, NZ)
            return c

        return lax.fori_loop(0, 4, body, carry, unroll=True)

    lax.fori_loop(0, 4, quarter, 0)
    lax.fori_loop(2, 4, z_inverse, 0)

    for c in small:
        c.wait_send()
    for c in same_half:
        c.wait_send()
    cross_own.wait_send()
    for d in range(1, TM):
        for j in range(4):
            window_send(j, other(d)).wait_send()
            end_send(j, other(d)).wait_send()
    for side in range(2):
        robin_send(side).wait()


def local(
    initial_state, heat_source, source_amplitude, diffusivity, robin_param,
    spectrum_x, spectrum_y, spectrum_z, robin_in, open_flag, owner_side,
):
    xf, yf, yi, xi, zf, zi = (jnp.asarray(c) for c in constants())
    hbm = pl.BlockSpec(memory_space=pltpu.HBM)
    dma = pltpu.SemaphoreType.DMA
    tile = (8, CB)
    return pl.pallas_call(
        sweep_kernel,
        out_shape=(
            pltpu.VMEM((1, 2, STEPS, 32, NZ), F32),
            pltpu.VMEM((1, NX, 32, NZ), F32),
        ),
        in_specs=[hbm] * 17,
        out_specs=(pl.BlockSpec(memory_space=pltpu.VMEM),) * 2,
        scratch_shapes=[
            pltpu.SMEM((STEPS,), F32), pltpu.SMEM((1,), F32), pltpu.SMEM((1,), F32),
            pltpu.SMEM((NX,), F32),
            pltpu.VMEM((1, 32), F32), pltpu.VMEM((1, NZ), F32),
            pltpu.VMEM((SPACE, 32), jnp.int32), pltpu.VMEM((SPACE, 32), jnp.int32),
            pltpu.VMEM(xf.shape, BF16), pltpu.VMEM(yf.shape, BF16), pltpu.VMEM(yi.shape, BF16),
            pltpu.VMEM(xi.shape, BF16), pltpu.VMEM(zi.shape, BF16),
            pltpu.VMEM((2, NX, 32, NZ), F32),
            pltpu.VMEM((NZ, 2 * CB), BF16),
            pltpu.VMEM((4, 2, NX) + tile, F32),
            pltpu.VMEM((2, 4, 2, NX) + tile, F32),
            pltpu.VMEM((2, 32, CB), F32),
            pltpu.VMEM((3,) + tile, F32),
            pltpu.VMEM((TM, STEPS) + tile, F32),
            pltpu.VMEM((2, STEPS, 32, NZ), F32),
            pltpu.VMEM((TM, 4, 2, STEPS) + tile, F32),
            pltpu.VMEM((2, 4, TM, 2, STEPS) + tile, F32),
            pltpu.VMEM((TM + 1, 4, 2, NX) + tile, F32),
            pltpu.VMEM((4, 2, NX) + tile, F32),
            pltpu.VMEM((4, 2, NX) + tile, F32),
            pltpu.VMEM((STEPS, 4) + tile, F32),
            pltpu.VMEM((4,) + tile, F32),
            pltpu.VMEM((TM, 4, 2, STEPS) + tile, F32),
            pltpu.VMEM((TM, 4, 2, STEPS) + tile, F32),
            pltpu.VMEM((2, STEPS, 32, NZ), F32),
            pltpu.VMEM((4, NX) + tile, F32),
            pltpu.VMEM((4, NX) + tile, F32),
            pltpu.VMEM((4, TM, NX) + tile, F32),
            pltpu.VMEM((4, TM, NX) + tile, F32),
            dma((13,)), dma((2, 4)), dma, dma((2,)), dma((TM,)), dma((TM,)), dma, dma,
            dma((4, TM)), dma((4, TM)),
            dma((4,)), dma((4,)), dma, dma, dma((2,)), dma((2,)), dma((TM,)), dma((TM,)),
            dma((4, TM)), dma((4, TM)), dma((4,)), dma((2,)), dma((2,)),
            dma((4, TM)), dma((4, TM)), dma((4,)),
        ],
        compiler_params=pltpu.CompilerParams(
            collective_id=0, has_side_effects=True, vmem_limit_bytes=44 << 20
        ),
        name="sweep",
    )(*(v if v.size == 1 else pltpu.with_memory_space_constraint(v, pltpu.HBM) for v in (
        initial_state, heat_source, robin_in, zf,
        source_amplitude, diffusivity, robin_param, spectrum_x,
        spectrum_y[None], spectrum_z[None], open_flag, owner_side,
        xf, yf, yi, xi, zi,
    )))


def solution(mesh):
    placed = (
        P("space", "cores", None),
        P("space", "cores", None),
        P("tm"),
        P("space"),
        P("space"),
        P(),
        P("cores"),
        P(),
        P("space", None, "tm", "cores", None),
        P(None, "cores"),
        P(None, "cores"),
    )
    return jax.shard_map(
        local,
        mesh=mesh,
        in_specs=placed,
        out_specs=(P("space", None, "tm", "cores", None), P("tm", "space", "cores", None)),
        check_vma=False,
    )
```

```python
import functools

import jax
import jax.numpy as jnp
import ml_dtypes
import numpy as np
from jax import lax
from jax.experimental import pallas as pl
from jax.experimental.pallas import tpu as pltpu
from jax.sharding import PartitionSpec as P

MESH = pl.DeviceIdType.MESH
F32, BF16 = jnp.float32, jnp.bfloat16
NX, NY, NZ, STEPS, TM, SPACE = 32, 64, 512, 8, 4, 32
CB = NZ // TM
LANES = CB // 4
PERM = list(range(0, NX, 2)) + list(range(1, NX, 2))


def cosine(n):
    k = np.arange(n)[:, None]
    i = np.arange(n)[None, :]
    scale = np.where(k == 0, np.sqrt(1.0 / n), np.sqrt(2.0 / n))
    return scale * np.cos(np.pi * k * (i + 0.5) / n)


C_X, C_Y, C_Z = cosine(NX), cosine(NY), cosine(NZ)
EDGE = C_X[PERM, 0]
VALUE_W = [float(v) for v in EDGE * EDGE]
SLOPE_W = [float(v) for v in (C_X[PERM, 1] - C_X[PERM, 0]) * EDGE]


def split_constant(m):
    hi = np.asarray(m, np.float32).astype(ml_dtypes.bfloat16)
    lo = (np.asarray(m, np.float64) - hi.astype(np.float64)).astype(np.float32)
    return np.stack([hi, lo.astype(ml_dtypes.bfloat16)])


def constants():
    eye8, eye4 = np.eye(8), np.eye(4)
    x_fwd = np.kron(C_X[PERM] / EDGE[:, None], eye8)
    x_inv = np.kron((C_X[PERM] * EDGE[:, None]).T, eye8)
    cy = C_Y.reshape(8, 8, 8, 8)
    y_fwd = np.einsum("pbqy,ac->pabqcy", cy, eye4).reshape(256, 256)
    y_inv = np.einsum("pbqy,ac->qaypcb", cy, eye4).reshape(2, 128, 256)
    y_inv = np.stack([split_constant(y_inv[0]), split_constant(y_inv[1])])
    z_fwd = split_constant(C_Z.T)
    z_fwd = z_fwd.reshape(2, NZ, TM, CB).transpose(2, 1, 0, 3).reshape(TM, NZ, 2 * CB)
    z_inv = split_constant(C_Z).reshape(2, TM, 4, LANES, NZ).transpose(0, 2, 1, 3, 4).reshape(2, 4, CB, NZ)
    z_inv = np.concatenate([z_inv[0], z_inv[0], z_inv[1]], axis=1)
    return (split_constant(x_fwd), split_constant(y_fwd), y_inv, split_constant(x_inv), z_fwd, z_inv)


def split(v):
    hi = v.astype(BF16)
    return hi, (v - hi.astype(F32)).astype(BF16)


def dot(a, b):
    return jnp.dot(a, b, preferred_element_type=F32)


def const_dot(m_hi, m_lo, v):
    hi, lo = split(v)
    return dot(m_hi, hi) + (dot(m_lo, hi) + dot(m_hi, lo))


def regroup(tiles):
    shape = tiles[0].shape
    t = [x.reshape(-1, CB) for x in tiles]
    lane = lax.broadcasted_iota(jnp.int32, t[0].shape, 1)
    low, even = lane < 64, lax.rem(lane, 64) < 32
    u = [None] * 4
    for a in (0, 1):
        u[a] = jnp.where(low, t[a], pltpu.roll(t[a + 2], 64, 1))
        u[a + 2] = jnp.where(low, pltpu.roll(t[a], 64, 1), t[a + 2])
    v = [None] * 4
    for a in (0, 2):
        v[a] = jnp.where(even, u[a], pltpu.roll(u[a + 1], 32, 1))
        v[a + 1] = jnp.where(even, pltpu.roll(u[a], 96, 1), u[a + 1])
    return [x.reshape(shape) for x in v]


def sweep_kernel(
    state_in, heat_in, robin_in, zf_in,
    amp_in, diff_in, param_in, specx_in, specy_in, specz_in, flag_in, owner_in,
    xf_in, yf_in, yi_in, xi_in, zi_in,
    robin_out, ends_out,
    amp_s, diff_s, param_s, specx_s, specy, specz, flag, owner,
    xf, yf, yi, xi, zi,
    xin, zf, vt, v, sycol, ptile, amp, rin, rp, rb, modes, src, fac, tr, coef, ob, st1, st,
    tbuf, xbuf, ubuf, wr,
    s_c, s_in, s_zf, s_rl, s_rs, r_rb, s_cw, r_cw, s_ro, r_ro, s_f, r_f, s_y, r_y, s_p, r_p, s_a, r_a,
    s_1, r_1, s_1l, s_o, r_o, s_w, r_w, s_wl,
):
    s = lax.axis_index("space")
    w = lax.axis_index("tm")
    h = lax.axis_index("cores")
    oh = 1 - h
    left = lax.rem(s + SPACE - 1, SPACE)
    right = lax.rem(s + 1, SPACE)

    def remote(a, b, ss, rs, to):
        return pltpu.make_async_remote_copy(
            src_ref=a, dst_ref=b, send_sem=ss, recv_sem=rs, device_id=to, device_id_type=MESH
        )

    def other(d):
        return lax.rem(w + d, TM)

    barrier = pltpu.get_barrier_semaphore()
    for d in range(1, TM):
        pl.semaphore_signal(barrier, inc=1, device_id=(s, other(d), h), device_id_type=MESH)
    for to in ((s, w, oh), (left, w, h), (right, w, h)):
        pl.semaphore_signal(barrier, inc=1, device_id=to, device_id_type=MESH)

    ins = (state_in, heat_in)
    own_robin = pltpu.make_async_copy(robin_in.at[0], rin, s_rl.at[0])
    own_robin.start()
    zf_copy = pltpu.make_async_copy(zf_in.at[w], zf, s_zf)
    zf_copy.start()
    operands = (
        (amp_in, amp_s), (param_in, param_s), (specy_in, specy), (xf_in, xf), (diff_in, diff_s),
        (specx_in, specx_s), (specz_in, specz), (flag_in, flag), (owner_in, owner),
        (yf_in, yf), (yi_in, yi), (xi_in, xi), (zi_in, zi),
    )
    loads = [pltpu.make_async_copy(a, b, s_c.at[i]) for i, (a, b) in enumerate(operands)]
    for c in loads[:4]:
        c.start()

    def load(i, yt):
        rows = pl.ds(pl.multiple_of(yt * 8, 8), 8)
        return pltpu.make_async_copy(ins[i].at[:, rows, :], xin.at[i, :, rows, :], s_in.at[i, yt])

    for yt in range(4):
        for i in range(2):
            load(i, yt).start()

    for c in loads[4:]:
        c.start()

    def column(row):
        n = row.shape[1]
        on = lax.broadcasted_iota(jnp.int32, (n, n), 0) == lax.broadcasted_iota(jnp.int32, (n, n), 1)
        picked = jnp.where(on, jnp.broadcast_to(row, (n, n)), 0.0)
        return jnp.broadcast_to(jnp.sum(picked, axis=1, keepdims=True), (n, CB))

    for c in loads[:3]:
        c.wait()
    for j in range(STEPS):
        amp[w, j] = jnp.full((8, CB), amp_s[j], F32)
    ptile[1] = jnp.full((8, CB), param_s[0], F32)
    sycol[h] = column(specy[...])
    own_robin.wait()

    def pack_robin(p, carry):
        lanes = pl.ds(pl.multiple_of(p * CB, CB), CB)
        for side in range(2):
            got = regroup([rin[side, :, pl.ds(8 * q, 8), lanes] for q in range(4)])
            for j in range(4):
                rp[p, j, side] = got[j]
        return carry

    pack_robin(w, 0)
    pl.semaphore_wait(barrier, 6)
    cross_own = remote(rp.at[w], rb.at[h, :, w], s_cw, r_cw, (s, w, oh))
    cross_own.start()
    keep_robin = pltpu.make_async_copy(rp.at[w], rb.at[h, :, w], s_rl.at[1])
    keep_robin.start()
    same_half = []
    for d in range(1, TM):
        pack_robin(other(d), 0)
        c = remote(rp.at[other(d)], rb.at[h, :, w], s_rs.at[d], r_rb.at[w], (s, other(d), h))
        c.start()
        same_half.append(c)

    def fwd_send(j):
        return remote(v.at[h, j], v.at[h, j], s_f.at[j], r_f.at[j], (s, w, oh))

    zf_copy.wait()
    loads[3].wait()

    def transform(yt, carry):
        rows = pl.ds(pl.multiple_of(yt * 8, 8), 8)
        zs = []
        for i in range(2):
            load(i, yt).wait()
            hi, lo = split(xin[i, :, rows, :].reshape(NX * 8, NZ))
            both = dot(hi, zf[...])
            zs.append(both[:, :CB] + (both[:, CB:] + dot(lo, zf[:, :CB])))
        res = const_dot(xf[0], xf[1], jnp.concatenate(zs, axis=1))
        vt[yt, 0] = res[:, :CB].reshape(NX, 8, CB)
        vt[yt, 1] = res[:, CB:].reshape(NX, 8, CB)
        return carry

    lax.fori_loop(0, 4, transform, 0, unroll=True)

    def pack_nodes(i, carry):
        at = pl.ds(pl.multiple_of(i * 8, 8), 8)
        for arr in range(2):
            got = regroup([vt[yt, arr, at] for yt in range(4)])
            for j in range(4):
                v[h, j, arr, at] = got[j]
        return carry

    lax.fori_loop(0, 4, pack_nodes, 0, unroll=True)
    for j in range(3):
        fwd_send(j).start()

    small = [
        remote(sycol.at[h], sycol.at[h], s_y, r_y, (s, w, oh)),
        remote(ptile.at[1], ptile.at[0], s_p.at[0], r_p.at[0], (right, w, h)),
        remote(ptile.at[1], ptile.at[2], s_p.at[1], r_p.at[1], (left, w, h)),
    ]
    for d in range(1, TM):
        small.append(remote(amp.at[w], amp.at[w], s_a.at[d], r_a.at[w], (s, other(d), h)))
    for c in small:
        c.start()

    for c in loads[4:9]:
        c.wait()
    remote(sycol.at[oh], sycol.at[oh], s_y, r_y, (s, w, oh)).wait_recv()
    small[1].wait_recv()
    small[2].wait_recv()

    def coefficient(at, here, beyond):
        opened = column(flag[pl.ds(at, 1), :].astype(F32))
        side = column(owner[pl.ds(at, 1), :].astype(F32))
        p = jnp.where(side > 0.5, beyond, here)
        return opened, opened * p

    pt = [jnp.broadcast_to(ptile[i][0:1], (32, CB)) for i in range(3)]
    o_l, op_l = coefficient(left, pt[0], pt[1])
    o_r, op_r = coefficient(s, pt[1], pt[2])
    for i, c in enumerate((o_l, op_l, o_r, op_r)):
        coef[i] = regroup([c[8 * q:8 * q + 8] for q in range(4)])[0]

    sz = jnp.broadcast_to(specz[:, pl.ds(pl.multiple_of(w * CB, CB), CB)], (8, CB))

    sz4 = regroup([sz] * 4)
    for half in range(2):
        sy = regroup([sycol[half, pl.ds(8 * q, 8), :] for q in range(4)])[0]

        def factor(a, carry):
            base = specx_s[a] + sy
            at = lax.div(a, 2) + lax.rem(a, 2) * (NX // 2)
            for j in range(4):
                fac[j, half, at] = 1.0 / (1.0 + diff_s[0] * (base + sz4[j]))
            return carry

        lax.fori_loop(0, NX, factor, 0)

    def clear(x, carry):
        ends_out[0, x] = jnp.zeros((32, NZ), F32)
        return carry

    lax.fori_loop(0, NX, clear, 0)

    keep_robin.wait()
    for d in range(1, TM):
        f = other(d)
        remote(rb.at[h, :, f], rb.at[h, :, f], s_rs.at[d], r_rb.at[f], (s, f, h)).wait_recv()
        remote(amp.at[f], amp.at[f], s_a.at[d], r_a.at[f], (s, f, h)).wait_recv()

    def cross(j, d):
        part = rb.at[h, j, other(d)]
        return remote(part, part, s_ro.at[j, d], r_ro.at[j, d], (s, w, oh))

    def cross_start(j):
        for d in range(1, TM):
            cross(j, d).start()

    for c in loads[9:]:
        c.wait()

    def y_forward(j):
        for i in range(2):
            def at(n):
                return pl.ds(16 * i + 4 * n, 4)

            sides = []
            for arr in range(2):
                rows = []
                for hh in range(2):
                    rows += regroup([v[hh, j, arr, at(n)] for n in range(4)])
                sides.append(jnp.concatenate([x.reshape(32, CB) for x in rows], axis=0))
            res = const_dot(yf[0], yf[1], jnp.concatenate(sides, axis=1))
            both = res.reshape(8, 4, 8, 2 * CB)
            for half in range(2):
                tiles = both[4 * half:4 * half + 4]
                got = regroup([tiles[q][:, :, :CB] for q in range(4)])
                for n in range(4):
                    modes[0, j, half, at(n)] = got[n]
                got = regroup([tiles[q][:, :, CB:] for q in range(4)])
                for n in range(4):
                    src[j, half, at(n)] = got[n]

    def steps(k, half, j, traces):
        for g in range(4):
            a0 = g * 8
            mu = [modes[k, j, half, a0 + i] for i in range(8)]
            fs = [fac[j, half, a0 + i] for i in range(8)]
            sg = [src[j, half, a0 + i] for i in range(8)]
            for t in range(STEPS):
                r0 = rb[half, j, k, 0, t]
                r1 = rb[half, j, k, 1, t]
                p = r0 + r1 if g < 2 else r0 - r1
                am = amp[k, t]
                for i in range(8):
                    mu[i] = (mu[i] + (am * sg[i] + p)) * fs[i]
                if traces:
                    val = [VALUE_W[a0 + i] * mu[i] for i in range(8)]
                    slo = [SLOPE_W[a0 + i] * mu[i] for i in range(8)]
                    val = sum(val[1:], val[0])
                    slo = sum(slo[1:], slo[0])
                    if g % 2 == 0:
                        tr[t, g] = val
                        tr[t, g + 1] = slo
                    elif g == 1:
                        tr[t, 0] += val
                        tr[t, 1] += slo
                    else:
                        e0, e1 = tr[t, 0], tr[t, 1]
                        o0 = tr[t, 2] + val
                        o1 = tr[t, 3] + slo
                        ob[k, j, 1, t] = coef[0] * (e1 + o1) + coef[1] * (e0 + o0)
                        ob[k, j, 0, t] = coef[3] * (e0 - o0) - coef[2] * (o1 - e1)
            for i in range(8):
                modes[k + 1, j, half, a0 + i] = mu[i]

    def window_send(j, k):
        return remote(ob.at[k, j], st1.at[w, j], s_1.at[j, k], r_1.at[j, w], (s, k, h))

    def window_keep(j):
        return pltpu.make_async_copy(ob.at[w, j], st1.at[w, j], s_1l.at[j])

    def own_quarter(j, carry):
        remote(v.at[oh, j], v.at[oh, j], s_f.at[j], r_f.at[j], (s, w, oh)).wait_recv()
        fwd_send(j).wait_send()

        @pl.when(j < 1)
        def _():
            fwd_send(j + 3).start()

        @pl.when(j >= 1)
        def _():
            cross_start(j - 1)

        y_forward(j)

        def own_steps(k, c):
            steps(k, h, j, True)
            return c

        lax.fori_loop(0, TM, own_steps, 0)
        for d in range(1, TM):
            window_send(j, other(d)).start()
        window_keep(j).start()
        return carry

    lax.fori_loop(0, 4, own_quarter, 0)

    def end_send(j, k):
        return remote(ubuf.at[j, k], wr.at[j, w], s_w.at[j, k], r_w.at[j, w], (s, k, h))

    def end_keep(j):
        return pltpu.make_async_copy(ubuf.at[j, w], wr.at[j, w], s_wl.at[j])

    def robin_send(side):
        return remote(
            st.at[side], robin_out.at[0, side], s_o.at[side], r_o.at[side],
            (jnp.where(side == 1, left, right), w, h),
        )

    def unpack_robin():
        for j in range(4):
            window_keep(j).wait()
            for d in range(1, TM):
                f = other(d)
                remote(ob.at[f, j], st1.at[f, j], s_1.at[j, f], r_1.at[j, f], (s, f, h)).wait_recv()

        def unpack(p, c):
            lanes = pl.ds(pl.multiple_of(p * CB, CB), CB)
            for side in range(2):
                got = regroup([st1[p, j, side] for j in range(4)])
                for q in range(4):
                    st[side, :, pl.ds(8 * q, 8), lanes] = got[q]
            return c

        lax.fori_loop(0, TM, unpack, 0)

    def quarter(j, carry):
        for d in range(1, TM):
            part = rb.at[oh, j, other(d)]
            remote(part, part, s_ro.at[j, d], r_ro.at[j, d], (s, w, oh)).wait_recv()
            cross(j, d).wait_send()

        @pl.when(j == 0)
        def _():
            remote(rp.at[w], rb.at[oh, :, w], s_cw, r_cw, (s, w, oh)).wait_recv()

        @pl.when(j < 1)
        def _():
            cross_start(j + 3)

        @pl.when(j == 1)
        def _():
            unpack_robin()

        @pl.when(j >= 2)
        def _():
            robin_send(j - 2).start()

        def body(k, c):
            steps(k, oh, j, False)
            return c

        lax.fori_loop(0, TM, body, 0)
        my_hi, my_lo = yi[h, 0], yi[h, 1]

        def y_inverse(g, c):
            at = pl.ds(pl.multiple_of(g * 8, 8), 8)
            tiles = []
            for half in range(2):
                tiles += regroup([modes[k + 1, j, half, at] for k in range(TM)])
            rhs = jnp.concatenate(
                [
                    jnp.concatenate([x[4 * i:4 * i + 4].reshape(32, CB) for x in tiles], axis=0)
                    for i in range(2)
                ],
                axis=1,
            )
            res = const_dot(my_hi, my_lo, rhs)
            tbuf[:, pl.ds(g * 8, 4)] = res[:, :CB].reshape(4, 4, 8, CB)
            tbuf[:, pl.ds(g * 8 + 4, 4)] = res[:, CB:].reshape(4, 4, 8, CB)
            return c

        lax.fori_loop(0, 4, y_inverse, 0, unroll=True)

        def x_inverse(q, c):
            rhs = jnp.concatenate(
                [tbuf[2 * q].reshape(256, CB), tbuf[2 * q + 1].reshape(256, CB)], axis=1
            )
            res = const_dot(xi[0], xi[1], rhs)
            xbuf[2 * q] = res[:, :CB].reshape(NX, 8, CB)
            xbuf[2 * q + 1] = res[:, CB:].reshape(NX, 8, CB)
            return c

        lax.fori_loop(0, 2, x_inverse, 0, unroll=True)

        def by_window(i, c):
            at = pl.ds(pl.multiple_of(i * 8, 8), 8)
            got = regroup([xbuf[yt, at] for yt in range(4)])
            for k in range(TM):
                ubuf[j, k, at] = got[k]
            return c

        for part in range(2):
            lax.fori_loop(2 * part, 2 * part + 2, by_window, 0, unroll=True)
            rows = pl.ds(16 * part, 16)
            for d in range(1, TM):
                k = other(d)
                remote(
                    ubuf.at[j, k, rows], wr.at[j, w, rows], s_w.at[j, k], r_w.at[j, w], (s, k, h)
                ).start()
        end_keep(j).start()

        @pl.when(j > 1)
        def _():
            z_inverse(j - 2, 0)

        return carry

    def z_inverse(j, carry):
        end_keep(j).wait()
        for d in range(1, TM):
            f = other(d)
            remote(ubuf.at[j, f], wr.at[j, f], s_w.at[j, f], r_w.at[j, f], (s, f, h)).wait_recv()

        def body(i, c):
            at = pl.ds(pl.multiple_of(i * 8, 8), 8)
            got = regroup([wr[j, p, at] for p in range(TM)])
            hi, lo = split(jnp.concatenate([x.reshape(64, CB) for x in got], axis=0))
            part = dot(jnp.concatenate([hi, lo], axis=1), zi[j, :2 * CB]) + dot(hi, zi[j, 2 * CB:])
            for yt in range(4):
                ends_out[0, at, pl.ds(8 * yt, 8), :] += part[64 * yt:64 * yt + 64].reshape(8, 8, NZ)
            return c

        return lax.fori_loop(0, 4, body, carry, unroll=True)

    lax.fori_loop(0, 4, quarter, 0)
    lax.fori_loop(2, 4, z_inverse, 0)

    for c in small:
        c.wait_send()
    for c in same_half:
        c.wait_send()
    cross_own.wait_send()
    for d in range(1, TM):
        for j in range(4):
            window_send(j, other(d)).wait_send()
            end_send(j, other(d)).wait_send()
    for side in range(2):
        robin_send(side).wait()


def local(
    initial_state, heat_source, source_amplitude, diffusivity, robin_param,
    spectrum_x, spectrum_y, spectrum_z, robin_in, open_flag, owner_side,
):
    xf, yf, yi, xi, zf, zi = (jnp.asarray(c) for c in constants())
    hbm = pl.BlockSpec(memory_space=pltpu.HBM)
    dma = pltpu.SemaphoreType.DMA
    tile = (8, CB)
    return pl.pallas_call(
        sweep_kernel,
        out_shape=(
            pltpu.VMEM((1, 2, STEPS, 32, NZ), F32),
            pltpu.VMEM((1, NX, 32, NZ), F32),
        ),
        in_specs=[hbm] * 17,
        out_specs=(pl.BlockSpec(memory_space=pltpu.VMEM),) * 2,
        scratch_shapes=[
            pltpu.SMEM((STEPS,), F32), pltpu.SMEM((1,), F32), pltpu.SMEM((1,), F32),
            pltpu.SMEM((NX,), F32),
            pltpu.VMEM((1, 32), F32), pltpu.VMEM((1, NZ), F32),
            pltpu.VMEM((SPACE, 32), jnp.int32), pltpu.VMEM((SPACE, 32), jnp.int32),
            pltpu.VMEM(xf.shape, BF16), pltpu.VMEM(yf.shape, BF16), pltpu.VMEM(yi.shape, BF16),
            pltpu.VMEM(xi.shape, BF16), pltpu.VMEM(zi.shape, BF16),
            pltpu.VMEM((2, NX, 32, NZ), F32),
            pltpu.VMEM((NZ, 2 * CB), BF16),
            pltpu.VMEM((4, 2, NX) + tile, F32),
            pltpu.VMEM((2, 4, 2, NX) + tile, F32),
            pltpu.VMEM((2, 32, CB), F32),
            pltpu.VMEM((3,) + tile, F32),
            pltpu.VMEM((TM, STEPS) + tile, F32),
            pltpu.VMEM((2, STEPS, 32, NZ), F32),
            pltpu.VMEM((TM, 4, 2, STEPS) + tile, F32),
            pltpu.VMEM((2, 4, TM, 2, STEPS) + tile, F32),
            pltpu.VMEM((TM + 1, 4, 2, NX) + tile, F32),
            pltpu.VMEM((4, 2, NX) + tile, F32),
            pltpu.VMEM((4, 2, NX) + tile, F32),
            pltpu.VMEM((STEPS, 4) + tile, F32),
            pltpu.VMEM((4,) + tile, F32),
            pltpu.VMEM((TM, 4, 2, STEPS) + tile, F32),
            pltpu.VMEM((TM, 4, 2, STEPS) + tile, F32),
            pltpu.VMEM((2, STEPS, 32, NZ), F32),
            pltpu.VMEM((4, NX) + tile, F32),
            pltpu.VMEM((4, NX) + tile, F32),
            pltpu.VMEM((4, TM, NX) + tile, F32),
            pltpu.VMEM((4, TM, NX) + tile, F32),
            dma((13,)), dma((2, 4)), dma, dma((2,)), dma((TM,)), dma((TM,)), dma, dma,
            dma((4, TM)), dma((4, TM)),
            dma((4,)), dma((4,)), dma, dma, dma((2,)), dma((2,)), dma((TM,)), dma((TM,)),
            dma((4, TM)), dma((4, TM)), dma((4,)), dma((2,)), dma((2,)),
            dma((4, TM)), dma((4, TM)), dma((4,)),
        ],
        compiler_params=pltpu.CompilerParams(
            collective_id=0, has_side_effects=True, vmem_limit_bytes=44 << 20
        ),
        name="sweep",
    )(*(v if v.size == 1 else pltpu.with_memory_space_constraint(v, pltpu.HBM) for v in (
        initial_state, heat_source, robin_in, zf,
        source_amplitude, diffusivity, robin_param, spectrum_x,
        spectrum_y[None], spectrum_z[None], open_flag, owner_side,
        xf, yf, yi, xi, zi,
    )))


def solution(mesh):
    placed = (
        P("space", "cores", None),
        P("space", "cores", None),
        P("tm"),
        P("space"),
        P("space"),
        P(),
        P("cores"),
        P(),
        P("space", None, "tm", "cores", None),
        P(None, "cores"),
        P(None, "cores"),
    )
    return jax.shard_map(
        local,
        mesh=mesh,
        in_specs=placed,
        out_specs=(P("space", None, "tm", "cores", None), P("tm", "space", "cores", None)),
        check_vma=False,
    )
```
